256 devices in a mesh: expert: 64 (over y, z, core), dp: 4 (over x).
Axes of the slice: x: 4, y: 4, z: 8, core: 2. Of those that a mesh axis runs over, the one named last changes fastest.
Arguments:
- grad_rows: bfloat16 [4, 32768, 2048], P('dp', 'expert'), may hold values from -6 to 6
- counts: int32 [4, 64, 64], P('dp', 'expert'), may hold values from 0 to 10, as said below
- order: int32 [4, 32768], P('dp', 'expert'), may hold values from 0 to 511, as said below
- hidden: bfloat16 [4, 64, 640, 768], P('dp', 'expert'), may hold values from -0.29882812 to 0.29882812
- down_weight: bfloat16 [64, 768, 2048], P('expert'), may hold values from -0.21875 to 0.21875
- error_in: bfloat16 [4, 64, 768, 2048], P('dp', 'expert'), may hold values from -6 to 6
- q_init: bfloat16 [64, 2048, 64], P('expert'), may hold values from -6 to 6
Outputs:
- input_grad: bfloat16 [4, 32768, 768], P('dp', 'expert')
- p_basis: float32 [64, 768, 64], P('expert')
- q_factor: float32 [64, 2048, 64], P('expert')
- error_out: bfloat16 [4, 64, 768, 2048], P('dp', 'expert')
The draws below stay inside these ranges and needn't reach their ends.
Inputs may be any that keep to these rules, and one draw needn't show every extreme that they name: On each device (r, s) the 64 counts sum to 512; in every draw one expert receives exactly 10 rows from every device. `order`: each device's 512 entries are a permutation of 0 to 511.
All inputs are finite; a program needn't handle non-finite values.
Results may differ from the reference program's by a relative error of at most 0.001.
Values may be sent and summed in bfloat16 or wider, within the bound.
A program may use at most 128 MiB of HBM per device.

```python
import jax
import jax.numpy as jnp
from jax import lax

D = 2048
FF = 768
RANK = 64
ROWS_DEV = 512
EXPERTS = 64
CAP = 10
N_EXPERT = 64
N_DP = 4


def draw_counts(key, part):
    mean_rows = ROWS_DEV // EXPERTS
    spread_rows = ROWS_DEV // (4 * EXPERTS)
    devices_all = N_DP * N_EXPERT
    key_one, key_two, key_three = jax.random.split(key, 3)
    chosen = jax.random.randint(key_one, (), 0, EXPERTS)
    device_keys = jax.random.split(key_two, devices_all)
    perms = jax.vmap(lambda one_key: jax.random.permutation(one_key, EXPERTS))(device_keys).astype(jnp.int32)
    where_chosen = jnp.argmax((perms == chosen).astype(jnp.int32), axis=1)
    device_ids = jnp.arange(devices_all)
    first_ids = perms[:, 0]
    perms = perms.at[device_ids, where_chosen].set(first_ids)
    perms = perms.at[:, 0].set(chosen)
    shifts = jax.random.randint(key_three, (devices_all, EXPERTS // 2), -spread_rows, spread_rows + 1)
    shifts = shifts.at[:, 0].set(spread_rows)
    result = jnp.zeros((devices_all, EXPERTS), jnp.int32)
    result = result.at[device_ids[:, None], perms[:, 0::2]].set(mean_rows + shifts)
    result = result.at[device_ids[:, None], perms[:, 1::2]].set(mean_rows - shifts)
    return result.reshape(N_DP, N_EXPERT, EXPERTS).astype(jnp.int32)


def draw_order(key, part):
    device_keys = jax.random.split(key, N_DP * N_EXPERT)
    perms = jax.vmap(lambda one_key: jax.random.permutation(one_key, ROWS_DEV))(device_keys)
    return perms.reshape(N_DP, N_EXPERT * ROWS_DEV).astype(jnp.int32)


def block_scale(key, extent, shards, smallest, top_value):
    factor_of, own = 1.0, jax.random.fold_in(key, 6)
    for axis_at, parts in shards:
        draws = jnp.exp(jax.random.uniform(jax.random.fold_in(own, axis_at), (parts,), jnp.float32, smallest / len(shards), top_value / len(shards)))
        factor_of = factor_of * jnp.repeat(draws, extent[axis_at] // parts).reshape([-1 if axis == axis_at else 1 for axis in range(len(extent))])
    return factor_of


def scatter_about(key, extent, deviation, bound, cuts=(), held_as=jnp.bfloat16):
    drawn = deviation * jax.random.normal(key, extent, jnp.float32)
    if cuts:
        drawn = drawn * block_scale(key, extent, cuts, -0.22, 0.18)
    return jnp.clip(drawn, -bound, bound).astype(held_as)


def setup_inputs(seed: int = 0) -> dict:
    streams_of = jax.random.split(jax.random.key(seed), 8)
    grad_rows = scatter_about(streams_of[0], (N_DP, N_EXPERT * ROWS_DEV, D), 1.0, 6.0, ((0, 4), (1, 64)))
    counts = draw_counts(jax.random.fold_in(streams_of[7], 71), 0)
    order = draw_order(jax.random.fold_in(streams_of[7], 71), 0)
    hidden = scatter_about(streams_of[3], (N_DP, EXPERTS, N_EXPERT * CAP, FF), 0.05, 0.29882812, ((0, 4), (1, 64)))
    down_weight = scatter_about(streams_of[4], (EXPERTS, FF, D), FF ** -0.5, 0.21875, ((0, 64),))
    error_in = scatter_about(streams_of[5], (N_DP, EXPERTS, FF, D), 1.0, 6.0, ((0, 4), (1, 64)))
    q_init = scatter_about(streams_of[6], (EXPERTS, D, RANK), 1.0, 6.0, ((0, 64),))
    return {"grad_rows": grad_rows, "counts": counts, "order": order, "hidden": hidden, "down_weight": down_weight, "error_in": error_in, "q_init": q_init}


def orthonormal(p_total):
    gram = jnp.dot(p_total.T, p_total, precision=lax.Precision.HIGHEST)
    lower = jnp.linalg.cholesky(gram)
    return lax.linalg.triangular_solve(lower, p_total, left_side=False, lower=True, transpose_a=True)

def reference(grad_rows, counts, order, hidden, down_weight, error_in, q_init):
    recv_rows = N_EXPERT * CAP
    route_ends = jnp.cumsum(counts, axis=2).astype(jnp.int32)
    route_starts = (route_ends - counts).astype(jnp.int32)
    slot_ids = jnp.arange(CAP, dtype=jnp.int32)
    source_ids = jnp.arange(N_EXPERT, dtype=jnp.int32)

    def one_expert(expert_id):
        start_now = route_starts[:, :, expert_id]
        count_now = counts[:, :, expert_id]
        pick_index = source_ids[None, :, None] * ROWS_DEV + start_now[:, :, None] + slot_ids[None, None, :]
        pick_index = jnp.minimum(pick_index, N_EXPERT * ROWS_DEV - 1).astype(jnp.int32)
        slot_valid = slot_ids[None, None, :] < count_now[:, :, None]
        picked = jax.vmap(lambda table, where_rows: table[where_rows])(grad_rows, pick_index.reshape(N_DP, recv_rows))
        picked = jnp.where(slot_valid.reshape(N_DP, recv_rows, 1), picked, jnp.zeros((), jnp.bfloat16))
        expert_weight = down_weight[expert_id]
        q_start = q_init[expert_id].astype(jnp.float32)
        back_list = []
        moment_list = []
        for replica in range(N_DP):
            saved_hidden = hidden[replica, expert_id]
            grad_w = jnp.dot(saved_hidden.T.astype(jnp.float32), picked[replica].astype(jnp.float32), preferred_element_type=jnp.float32)
            back_list.append(jnp.dot(picked[replica].astype(jnp.float32), expert_weight.T.astype(jnp.float32), preferred_element_type=jnp.float32).astype(jnp.bfloat16))
            moment_list.append(grad_w + error_in[replica, expert_id].astype(jnp.float32))
        p_total = jnp.dot(moment_list[0], q_start, precision=lax.Precision.HIGHEST)
        for replica in range(1, N_DP):
            p_total = p_total + jnp.dot(moment_list[replica], q_start, precision=lax.Precision.HIGHEST)
        p_basis = orthonormal(p_total)
        q_total = jnp.dot(moment_list[0].T, p_basis, precision=lax.Precision.HIGHEST)
        for replica in range(1, N_DP):
            q_total = q_total + jnp.dot(moment_list[replica].T, p_basis, precision=lax.Precision.HIGHEST)
        q_factor = q_total / N_DP
        approximation = jnp.dot(p_basis, q_factor.T, precision=lax.Precision.HIGHEST)
        errors = jnp.stack([(moment - approximation).astype(jnp.bfloat16) for moment in moment_list])
        return (jnp.stack(back_list), p_basis, q_factor, errors)
    backs, bases, q_factors, errors = lax.map(one_expert, jnp.arange(EXPERTS, dtype=jnp.int32))
    flat_back = backs.reshape(EXPERTS * N_DP * recv_rows, FF)
    source_pos = order.reshape(N_DP, N_EXPERT, ROWS_DEV)
    expert_of = jnp.sum((route_ends[:, :, None, :] <= source_pos[:, :, :, None]).astype(jnp.int32), axis=3).astype(jnp.int32)
    start_of = jnp.take_along_axis(route_starts, expert_of, axis=2)
    replica_ids = jnp.arange(N_DP, dtype=jnp.int32)[:, None, None]
    owner_ids = jnp.arange(N_EXPERT, dtype=jnp.int32)[None, :, None]
    position = (expert_of * N_DP + replica_ids) * recv_rows + owner_ids * CAP + source_pos - start_of
    input_grad = flat_back[position.reshape(-1).astype(jnp.int32)].reshape(N_DP, N_EXPERT * ROWS_DEV, FF)
    return (input_grad, bases, q_factors, jnp.transpose(errors, (1, 0, 2, 3)))
```

```python
import jax
import jax.numpy as jnp
from jax import lax
from jax.experimental import pallas as pl
from jax.experimental.pallas import tpu as pltpu
from jax.sharding import PartitionSpec as P

MESH = pl.DeviceIdType.MESH
F32 = jnp.float32
BF16 = jnp.bfloat16

NY, NZ, NC, NDP = 4, 8, 2, 4
ROWS, D, FF, RANK, EXPERTS = 512, 2048, 768, 64, 64
GROUPS, MEMBERS = 8, 8
GROUP_ROWS = 80
WIDE = D + 512
BACK = FF + 256
BLOCK = D // NDP
P_ROWS = RANK // NDP


def nn(a, b, precision=None):
    return lax.dot_general(
        a, b, (((1,), (0,)), ((), ())), precision=precision, preferred_element_type=F32
    )


def nt(a, b, precision=None):
    return lax.dot_general(
        a, b, (((1,), (1,)), ((), ())), precision=precision, preferred_element_type=F32
    )


def split(a):
    high = a.astype(BF16)
    return high, (a - high.astype(F32)).astype(BF16)


def onehot(mask):
    return jnp.where(mask, 1.0, 0.0).astype(BF16)


def iota(shape, axis):
    return lax.broadcasted_iota(jnp.int32, shape, axis)


def z_step(k):
    half = (k + 1) // 2
    return 4 + (1 - 2 * (k % 2)) * half


def shift(y, z, c, k, m, sign):
    there_y = (y + sign * (m // 2) + NY) % NY
    there_z = (z + sign * z_step(k) + NZ) % NZ
    there_c = (c + m % 2) % NC
    return (there_y * NZ + there_z) * NC + there_c


def group_codes(y, z, c, k, sign, scale):
    main = iota((64, 1), 0)
    tail = iota((16, 1), 0)
    main_code = shift(y, z, c, k, main // 8, sign) * scale + main % 8
    tail_code = shift(y, z, c, k, tail // 2, sign) * scale + 8 + tail % 2
    return main_code, tail_code


def routes(ends, rows):
    passed = ends <= rows
    expert = jnp.sum(jnp.where(passed, 1.0, 0.0), axis=0, keepdims=True)
    start = jnp.max(jnp.where(passed, ends, 0.0), axis=0, keepdims=True)
    return expert * 16.0 + (rows - start)


def inverse_factor(gram):
    lanes = iota((RANK, 2 * RANK), 1)
    rows = iota((RANK, 2 * RANK), 0)
    work = jnp.concatenate([gram, jnp.where(iota((RANK, RANK), 0) == iota((RANK, RANK), 1), 1.0, 0.0)], axis=1)
    blocks = [work[8 * b : 8 * b + 8] for b in range(8)]
    below = iota((8, 1), 0)
    for k in range(RANK):
        own, at = k // 8, k % 8
        row = blocks[own][at : at + 1, :]
        scaled = row / row[:, k : k + 1]
        for b in range(own, 8):
            factor = blocks[b][:, k : k + 1]
            if b == own:
                factor = jnp.where(below > at, factor, 0.0)
            blocks[b] = blocks[b] - factor * scaled
    work = jnp.concatenate(blocks, axis=0)
    pivots = jnp.sum(jnp.where(lanes == rows, work, 0.0), axis=1, keepdims=True)
    return work[:, RANK:] * lax.rsqrt(pivots)


def kernel(
    x_hbm, counts_ref, order_ref, hidden_hbm, weight_hbm, error_hbm, q_ref,
    back_out, p_out, q_out, error_out,
    x, hidden, weight, error, send, recv, held, hidden_p, hidden_t, moment, moment_h, moment_l,
    pick, back_send, back_recv, back_rows, p_part, p_recv, p_full, z_part, z_recv, q_full,
    error_new, factor_t, load_sem, store_sem, send_sem, recv_sem, back_send_sem, back_recv_sem,
    p_sem, g_sem, z_sem, q_sem, own_sem,
):
    me = lax.axis_index("expert")
    replica = lax.axis_index("dp")
    y, z, c = me // (NZ * NC), (me // NC) % NZ, me % NC

    loads = [
        pltpu.make_async_copy(src, dst, load_sem.at[i])
        for i, (src, dst) in enumerate(
            [(x_hbm, x), (hidden_hbm, hidden), (error_hbm, error), (weight_hbm, weight)]
        )
    ]
    for load in loads:
        load.start()

    barrier = pltpu.get_barrier_semaphore()

    @pl.loop(1, EXPERTS)
    def _(k):
        pl.semaphore_signal(
            barrier, inc=1, device_id={"expert": (me + k) % EXPERTS}, device_id_type=MESH
        )

    for i in range(1, NDP):
        pl.semaphore_signal(
            barrier, inc=1, device_id={"dp": (replica + i) % NDP}, device_id_type=MESH
        )

    counts = counts_ref[...].astype(F32)
    ends = jnp.sum(
        jnp.where(iota((EXPERTS, EXPERTS), 1) <= iota((EXPERTS, EXPERTS), 0), counts, 0.0),
        axis=1,
        keepdims=True,
    )
    codes = routes(ends, iota((1, ROWS), 1).astype(F32))
    loads[0].wait()

    def forward(k, m):
        return pltpu.make_async_remote_copy(
            src_ref=send.at[k, m],
            dst_ref=recv.at[k, m],
            send_sem=send_sem.at[k, m],
            recv_sem=recv_sem.at[k, m],
            device_id={"expert": shift(y, z, c, k, m, 1)},
            device_id_type=MESH,
        )

    def backward(k, m):
        return pltpu.make_async_remote_copy(
            src_ref=back_send.at[k, m],
            dst_ref=back_recv.at[k, m],
            send_sem=back_send_sem.at[k, m],
            recv_sem=back_recv_sem.at[k, m],
            device_id={"expert": shift(y, z, c, k, m, -1)},
            device_id_type=MESH,
        )

    def pack(k):
        rows = iota((64, 1), 0)
        expert = shift(y, z, c, k, rows // 8, 1) * 16
        main = onehot(codes == (expert + rows % 8).astype(F32))
        tail = codes == (expert + 8 + rows % 2).astype(F32)
        part = (rows % 8) // 2
        total = jnp.zeros((64, 512), F32)
        for i in range(4):
            columns = x[:, 512 * i : 512 * i + 512]
            both = nn(
                jnp.concatenate([main, onehot(tail & (part == i))], axis=0), columns
            )
            send[k, :, :, 512 * i : 512 * i + 512] = both[:64].reshape(8, 8, 512).astype(BF16)
            total = total + both[64:]
        send[k, :, :, D:] = total.reshape(8, 8, 512).astype(BF16)

    pack(0)
    pl.semaphore_wait(barrier, EXPERTS - 1 + NDP - 1)
    for m in range(MEMBERS):
        forward(0, m).start()

    @pl.loop(1, GROUPS - 1)
    def _(k):
        pack(k)
        for m in range(MEMBERS):
            forward(k, m).start()

    pack(GROUPS - 1)
    for m in range(1, MEMBERS):
        forward(GROUPS - 1, m).start()
    own = pltpu.make_async_copy(send.at[GROUPS - 1, 0], recv.at[GROUPS - 1, 0], own_sem.at[0])
    own.start()

    loads[1].wait()

    @pl.loop(0, GROUPS)
    def _(k):
        main_code, tail_code = group_codes(y, z, c, k, -1, 10)
        code = jnp.concatenate([main_code, tail_code], axis=0)
        rows = pl.ds(pl.multiple_of(k * GROUP_ROWS, 16), GROUP_ROWS)
        hidden_p[rows, :] = nn(onehot(iota((GROUP_ROWS, 640), 1) == code), hidden[...]).astype(BF16)

    for i in range(FF // 128):
        hidden_t[128 * i : 128 * i + 128, :] = (
            hidden_p[:, 128 * i : 128 * i + 128].astype(F32).T.astype(BF16)
        )
    wanted = routes(ends, order_ref[...].astype(F32))

    for k in range(GROUPS):
        main_code, tail_code = group_codes(y, z, c, k, 1, 16)
        code = jnp.concatenate([main_code, tail_code], axis=0).astype(F32)
        pick[k * GROUP_ROWS : (k + 1) * GROUP_ROWS, :] = onehot(wanted == code)

    q = q_ref[...]
    loads[2].wait()
    for i in range(3):
        p_part[:, 256 * i : 256 * i + 256] = nt(q, error[256 * i : 256 * i + 256, :])
    loads[3].wait()

    spread = iota((16, 64), 1)
    gathered = iota((16, 64), 0)

    def unpack(ref, k, width, parts, size):
        block = ref[k].astype(F32).reshape(64, width + size)
        main = block[:, :width].astype(BF16)
        tail = block[:, width:].astype(BF16)
        pieces = []
        for i in range(parts):
            at = (gathered // 2) * 8 + 2 * i + gathered % 2
            pieces.append(nn(onehot(spread == at), tail).astype(BF16))
        return main, jnp.concatenate(pieces, axis=1)

    def take(k):
        rows = pl.ds(pl.multiple_of(k * GROUP_ROWS, 16), GROUP_ROWS)
        main, tail = unpack(recv, k, D, 4, 512)
        mine = jnp.concatenate([main, tail], axis=0)
        held[rows, :] = mine
        high, low = split(nt(q, mine))
        both = nn(jnp.concatenate([high, low], axis=0), hidden_p[rows, :])
        p_part[...] += both[:RANK] + both[RANK:]

    def answer(k):
        rows = pl.ds(pl.multiple_of(k * GROUP_ROWS, 16), GROUP_ROWS)
        mine = held[rows, :]
        for i in range(3):
            columns = slice(256 * i, 256 * i + 256)
            slot = nt(mine, weight[columns, :])
            back_send[k, :, :, columns] = slot[:64].reshape(8, 8, 256).astype(BF16)
            tail = slot[64:].astype(BF16)
            to = iota((64, 16), 0)
            at = (to // 8) * 2 + to % 2
            mask = (iota((64, 16), 1) == at) & ((to % 8) // 2 == i)
            placed = nn(onehot(mask), tail)
            if i == 0:
                total = placed
            else:
                total = total + placed
        back_send[k, :, :, FF:] = total.reshape(8, 8, 256).astype(BF16)

    @pl.loop(0, GROUPS - 1)
    def _(k):
        for m in range(MEMBERS):
            forward(k, m).wait_recv()
        take(k)
        answer(k)

    for m in range(1, MEMBERS):
        forward(GROUPS - 1, m).wait_recv()
    own.wait()
    take(GROUPS - 1)

    def p_scatter(i):
        peer = (replica + i) % NDP
        return pltpu.make_async_remote_copy(
            src_ref=p_part.at[pl.ds(pl.multiple_of(peer * P_ROWS, 8), P_ROWS)],
            dst_ref=p_recv.at[i - 1],
            send_sem=p_sem.at[0, i - 1],
            recv_sem=p_sem.at[1, i - 1],
            device_id={"dp": peer},
            device_id_type=MESH,
        )

    my_rows = pl.ds(pl.multiple_of(replica * P_ROWS, 8), P_ROWS)

    def p_gather(i):
        return pltpu.make_async_remote_copy(
            src_ref=p_full.at[my_rows],
            dst_ref=p_full.at[my_rows],
            send_sem=g_sem.at[0, i - 1],
            recv_sem=g_sem.at[1, i - 1],
            device_id={"dp": (replica + i) % NDP},
            device_id_type=MESH,
        )

    for i in range(1, NDP):
        p_scatter(i).start()
    answer(GROUPS - 1)
    for i in range(1, NDP):
        p_scatter(i).wait_recv()
    p_full[my_rows, :] = p_part[my_rows, :] + p_recv[0] + p_recv[1] + p_recv[2]
    for i in range(1, NDP):
        p_gather(i).start()

    @pl.loop(0, GROUPS - 1)
    def _(k):
        for m in range(MEMBERS):
            backward(k, m).start()

    for m in range(1, MEMBERS):
        backward(GROUPS - 1, m).start()
    own_back = pltpu.make_async_copy(
        back_send.at[GROUPS - 1, 0], back_recv.at[GROUPS - 1, 0], own_sem.at[1]
    )
    own_back.start()

    @pl.loop(0, D // 256)
    def _(i):
        columns = pl.ds(pl.multiple_of(i * 256, 256), 256)
        value = nn(hidden_t[...], held[:, columns]) + error[:, columns].astype(F32)
        moment[:, columns] = value
        high, low = split(value)
        moment_h[:, columns] = high
        moment_l[:, columns] = low

    for i in range(1, NDP):
        p_gather(i).wait_recv()

    total = p_full[...]
    total_h, total_l = split(total)
    total_both = jnp.concatenate([total_h, total_l], axis=0)

    def z_scatter(i):
        peer = (replica + i) % NDP
        return pltpu.make_async_remote_copy(
            src_ref=z_part.at[i],
            dst_ref=z_recv.at[i - 1],
            send_sem=z_sem.at[0, i - 1],
            recv_sem=z_sem.at[1, i - 1],
            device_id={"dp": peer},
            device_id_type=MESH,
        )

    for i in (2, 1, 3, 0):
        block = pl.ds(pl.multiple_of(((replica + i) % NDP) * BLOCK, BLOCK), BLOCK)
        both = nn(total_both, moment_h[:, block])
        z_part[i] = both[:RANK] + both[RANK:] + nn(total_h, moment_l[:, block])
        if i:
            z_scatter(i).start()

    gram = nt(total, total, lax.Precision.HIGHEST)
    inverse = inverse_factor(gram)
    basis = nn(inverse, total, lax.Precision.HIGHEST)
    p_out[...] = basis
    basis_h, basis_l = split(basis)
    three = jnp.concatenate([basis_h, basis_l, basis_h], axis=0).astype(F32)
    for i in range(FF // 128):
        factor_t[128 * i : 128 * i + 128, :] = three[:, 128 * i : 128 * i + 128].T.astype(BF16)

    for i in range(1, NDP):
        z_scatter(i).wait_recv()
    z_total = z_part[0] + z_recv[0] + z_recv[1] + z_recv[2]
    q_full[replica] = nn(inverse, z_total, lax.Precision.HIGHEST) / NDP

    def q_gather(i):
        return pltpu.make_async_remote_copy(
            src_ref=q_full.at[replica],
            dst_ref=q_full.at[replica],
            send_sem=q_sem.at[0, i - 1],
            recv_sem=q_sem.at[1, i - 1],
            device_id={"dp": (replica + i) % NDP},
            device_id_type=MESH,
        )

    for i in range(1, NDP):
        q_gather(i).start()

    def store(i):
        block = pl.ds(pl.multiple_of(((replica + NDP - i) % NDP) * BLOCK, BLOCK), BLOCK)
        return pltpu.make_async_copy(error_new.at[i], error_out.at[:, block], store_sem.at[i])

    for i in (0, 1, 3, 2):
        if i:
            q_gather(i).wait_recv()
        owner = (replica + NDP - i) % NDP
        block = pl.ds(pl.multiple_of(owner * BLOCK, BLOCK), BLOCK)
        part = q_full[owner]
        q_out[:, block] = part
        part_h, part_l = split(part)
        part_three = jnp.concatenate([part_h, part_h, part_l], axis=0)
        for j in range(3):
            rows = slice(256 * j, 256 * j + 256)
            error_new[i, rows, :] = (
                moment[rows, block] - nn(factor_t[rows, :], part_three)
            ).astype(BF16)
        store(i).start()

    own_back.wait()

    @pl.loop(0, GROUPS - 1)
    def _(k):
        for m in range(MEMBERS):
            backward(k, m).wait_recv()
        rows = pl.ds(pl.multiple_of(k * GROUP_ROWS, 16), GROUP_ROWS)
        main, tail = unpack(back_recv, k, FF, 3, 256)
        back_rows[rows, :] = jnp.concatenate([main, tail], axis=0)

    for m in range(1, MEMBERS):
        backward(GROUPS - 1, m).wait_recv()
    main, tail = unpack(back_recv, GROUPS - 1, FF, 3, 256)
    back_rows[(GROUPS - 1) * GROUP_ROWS :, :] = jnp.concatenate([main, tail], axis=0)
    for i in range(4):
        chosen = lax.dot_general(
            pick[:, 128 * i : 128 * i + 128],
            back_rows[...],
            (((0,), (0,)), ((), ())),
            preferred_element_type=F32,
        )
        back_out[128 * i : 128 * i + 128, :] = chosen.astype(BF16)

    for i in range(NDP):
        store(i).wait()
    for i in range(1, NDP):
        p_scatter(i).wait_send()
        p_gather(i).wait_send()
        z_scatter(i).wait_send()
        q_gather(i).wait_send()

    @pl.loop(0, GROUPS - 1)
    def _(k):
        for m in range(MEMBERS):
            forward(k, m).wait_send()
            backward(k, m).wait_send()

    for m in range(1, MEMBERS):
        forward(GROUPS - 1, m).wait_send()
        backward(GROUPS - 1, m).wait_send()


def shards(grad_rows, counts, order, hidden, down_weight, error_in, q_init):
    anywhere = pl.BlockSpec(memory_space=pl.ANY)
    vmem = pl.BlockSpec(memory_space=pltpu.VMEM)
    dma = pltpu.SemaphoreType.DMA
    back, basis, factor, error_new = pl.pallas_call(
        kernel,
        out_shape=(
            jax.ShapeDtypeStruct((ROWS, FF), BF16),
            jax.ShapeDtypeStruct((RANK, FF), F32),
            jax.ShapeDtypeStruct((RANK, D), F32),
            jax.ShapeDtypeStruct((FF, D), BF16),
        ),
        in_specs=[anywhere, vmem, vmem, anywhere, anywhere, anywhere, vmem],
        out_specs=(vmem, vmem, vmem, anywhere),
        scratch_shapes=[
            pltpu.VMEM((ROWS, D), BF16),
            pltpu.VMEM((640, FF), BF16),
            pltpu.VMEM((FF, D), BF16),
            pltpu.VMEM((FF, D), BF16),
            pltpu.VMEM((GROUPS, MEMBERS, 8, WIDE), BF16),
            pltpu.VMEM((GROUPS, MEMBERS, 8, WIDE), BF16),
            pltpu.VMEM((640, D), BF16),
            pltpu.VMEM((640, FF), BF16),
            pltpu.VMEM((FF, 640), BF16),
            pltpu.VMEM((FF, D), F32),
            pltpu.VMEM((FF, D), BF16),
            pltpu.VMEM((FF, D), BF16),
            pltpu.VMEM((640, ROWS), BF16),
            pltpu.VMEM((GROUPS, MEMBERS, 8, BACK), BF16),
            pltpu.VMEM((GROUPS, MEMBERS, 8, BACK), BF16),
            pltpu.VMEM((640, FF), BF16),
            pltpu.VMEM((RANK, FF), F32),
            pltpu.VMEM((NDP - 1, P_ROWS, FF), F32),
            pltpu.VMEM((RANK, FF), F32),
            pltpu.VMEM((NDP, RANK, BLOCK), F32),
            pltpu.VMEM((NDP - 1, RANK, BLOCK), F32),
            pltpu.VMEM((NDP, RANK, BLOCK), F32),
            pltpu.VMEM((NDP, FF, BLOCK), BF16),
            pltpu.VMEM((FF, 3 * RANK), BF16),
            dma((4,)),
            dma((NDP,)),
            dma((GROUPS, MEMBERS)),
            dma((GROUPS, MEMBERS)),
            dma((GROUPS, MEMBERS)),
            dma((GROUPS, MEMBERS)),
            dma((2, NDP - 1)),
            dma((2, NDP - 1)),
            dma((2, NDP - 1)),
            dma((2, NDP - 1)),
            dma((2,)),
        ],
        compiler_params=pltpu.CompilerParams(
            collective_id=0, has_side_effects=True, vmem_limit_bytes=58 << 20
        ),
        name="routed_backward",
    )(
        grad_rows[0],
        counts[0],
        order,
        hidden[0, 0],
        down_weight[0],
        error_in[0, 0],
        q_init[0].T,
    )
    return back[None], basis.T[None], factor.T[None], error_new[None, None]


def solution(mesh):
    placed = (
        P("dp", "expert", None),
        P("dp", "expert", None),
        P("dp", "expert"),
        P("dp", "expert", None, None),
        P("expert", None, None),
        P("dp", "expert", None, None),
        P("expert", None, None),
    )
    return jax.shard_map(
        shards,
        mesh=mesh,
        in_specs=placed,
        out_specs=(
            P("dp", "expert", None),
            P("expert", None, None),
            P("expert", None, None),
            P("dp", "expert", None, None),
        ),
        check_vma=False,
    )
```

```python
import jax
import jax.numpy as jnp
from jax import lax
from jax.experimental import pallas as pl
from jax.experimental.pallas import tpu as pltpu
from jax.sharding import PartitionSpec as P

MESH = pl.DeviceIdType.MESH
F32 = jnp.float32
BF16 = jnp.bfloat16

NY, NZ, NC, NDP = 4, 8, 2, 4
ROWS, D, FF, RANK, EXPERTS = 512, 2048, 768, 64, 64
GROUPS, MEMBERS = 8, 8
GROUP_ROWS = 80
WIDE = D + 512
BACK = FF + 256
BLOCK = D // NDP
P_ROWS = RANK // NDP


def nn(a, b, precision=None):
    return lax.dot_general(
        a, b, (((1,), (0,)), ((), ())), precision=precision, preferred_element_type=F32
    )


def nt(a, b, precision=None):
    return lax.dot_general(
        a, b, (((1,), (1,)), ((), ())), precision=precision, preferred_element_type=F32
    )


def split(a):
    high = a.astype(BF16)
    return high, (a - high.astype(F32)).astype(BF16)


def onehot(mask):
    return jnp.where(mask, 1.0, 0.0).astype(BF16)


def iota(shape, axis):
    return lax.broadcasted_iota(jnp.int32, shape, axis)


def z_step(m):
    half = (m + 1) // 2
    return 4 + (1 - 2 * (m % 2)) * half


def shift(y, z, c, k, m, sign):
    there_y = (y + sign * ((k // 2 + m + 2) % NY) + NY) % NY
    there_z = (z + sign * z_step(m) + NZ) % NZ
    there_c = (c + k + 1) % NC
    return (there_y * NZ + there_z) * NC + there_c


def group_codes(y, z, c, k, sign, scale):
    main = iota((64, 1), 0)
    tail = iota((16, 1), 0)
    main_code = shift(y, z, c, k, main // 8, sign) * scale + main % 8
    tail_code = shift(y, z, c, k, tail // 2, sign) * scale + 8 + tail % 2
    return main_code, tail_code


def routes(ends, rows):
    passed = ends <= rows
    expert = jnp.sum(jnp.where(passed, 1.0, 0.0), axis=0, keepdims=True)
    start = jnp.max(jnp.where(passed, ends, 0.0), axis=0, keepdims=True)
    return expert * 16.0 + (rows - start)


def inverse_factor(gram):
    lanes = iota((RANK, 2 * RANK), 1)
    rows = iota((RANK, 2 * RANK), 0)
    work = jnp.concatenate([gram, jnp.where(iota((RANK, RANK), 0) == iota((RANK, RANK), 1), 1.0, 0.0)], axis=1)
    blocks = [work[8 * b : 8 * b + 8] for b in range(8)]
    below = iota((8, 1), 0)
    for k in range(RANK):
        own, at = k // 8, k % 8
        row = blocks[own][at : at + 1, :]
        scaled = row / row[:, k : k + 1]
        for b in range(own, 8):
            factor = blocks[b][:, k : k + 1]
            if b == own:
                factor = jnp.where(below > at, factor, 0.0)
            blocks[b] = blocks[b] - factor * scaled
    work = jnp.concatenate(blocks, axis=0)
    pivots = jnp.sum(jnp.where(lanes == rows, work, 0.0), axis=1, keepdims=True)
    return work[:, RANK:] * lax.rsqrt(pivots)


def kernel(
    x_hbm, counts_ref, order_ref, hidden_hbm, weight_hbm, error_hbm, q_ref,
    back_rows, p_out, q_full, moment_out, pick_out, factor_out,
    x, hidden, weight, error, send, recv, held, hidden_p, hidden_t, moment, moment_h, moment_l,
    pick, back_send, back_recv, p_part, p_recv, p_full, z_part, z_recv, factor_t, load_sem, store_sem, send_sem, recv_sem, back_send_sem, back_recv_sem,
    p_sem, g_sem, z_sem, q_sem, own_sem,
):
    me = lax.axis_index("expert")
    replica = lax.axis_index("dp")
    y, z, c = me // (NZ * NC), (me // NC) % NZ, me % NC

    loads = [
        pltpu.make_async_copy(src, dst, load_sem.at[i])
        for i, (src, dst) in enumerate(
            [(x_hbm, x), (hidden_hbm, hidden), (error_hbm, error), (weight_hbm, weight)]
        )
    ]
    for load in loads:
        load.start()

    barrier = pltpu.get_barrier_semaphore()

    @pl.loop(1, EXPERTS)
    def _(k):
        pl.semaphore_signal(
            barrier, inc=1, device_id={"expert": (me + k) % EXPERTS}, device_id_type=MESH
        )

    for i in range(1, NDP):
        pl.semaphore_signal(
            barrier, inc=1, device_id={"dp": (replica + i) % NDP}, device_id_type=MESH
        )

    counts = counts_ref[...].astype(F32)
    ends = jnp.sum(
        jnp.where(iota((EXPERTS, EXPERTS), 1) <= iota((EXPERTS, EXPERTS), 0), counts, 0.0),
        axis=1,
        keepdims=True,
    )
    codes = routes(ends, iota((1, ROWS), 1).astype(F32))
    loads[0].wait()

    def forward(k, m):
        return pltpu.make_async_remote_copy(
            src_ref=send.at[k, m],
            dst_ref=recv.at[k, m],
            send_sem=send_sem.at[k, m],
            recv_sem=recv_sem.at[k, m],
            device_id={"expert": shift(y, z, c, k, m, 1)},
            device_id_type=MESH,
        )

    def backward(k, m):
        return pltpu.make_async_remote_copy(
            src_ref=back_send.at[k, m],
            dst_ref=back_recv.at[k, m],
            send_sem=back_send_sem.at[k, m],
            recv_sem=back_recv_sem.at[k, m],
            device_id={"expert": shift(y, z, c, k, m, -1)},
            device_id_type=MESH,
        )

    def pack(k):
        rows = iota((64, 1), 0)
        expert = shift(y, z, c, k, rows // 8, 1) * 16
        main = onehot(codes == (expert + rows % 8).astype(F32))
        tail = codes == (expert + 8 + rows % 2).astype(F32)
        part = (rows % 8) // 2
        total = jnp.zeros((64, 512), F32)
        for i in range(4):
            columns = x[:, 512 * i : 512 * i + 512]
            both = nn(
                jnp.concatenate([main, onehot(tail & (part == i))], axis=0), columns
            )
            send[k, :, :, 512 * i : 512 * i + 512] = both[:64].reshape(8, 8, 512).astype(BF16)
            total = total + both[64:]
        send[k, :, :, D:] = total.reshape(8, 8, 512).astype(BF16)

    pack(0)
    pl.semaphore_wait(barrier, EXPERTS - 1 + NDP - 1)
    for m in range(MEMBERS):
        forward(0, m).start()

    @pl.loop(1, GROUPS - 1)
    def _(k):
        pack(k)
        for m in range(MEMBERS):
            forward(k, m).start()

    pack(GROUPS - 1)
    for m in range(MEMBERS - 1):
        forward(GROUPS - 1, m).start()
    own = pltpu.make_async_copy(send.at[GROUPS - 1, MEMBERS - 1], recv.at[GROUPS - 1, MEMBERS - 1], own_sem.at[0])
    own.start()

    loads[1].wait()

    @pl.loop(0, GROUPS)
    def _(k):
        main_code, tail_code = group_codes(y, z, c, k, -1, 10)
        code = jnp.concatenate([main_code, tail_code], axis=0)
        rows = pl.ds(pl.multiple_of(k * GROUP_ROWS, 16), GROUP_ROWS)
        hidden_p[rows, :] = nn(onehot(iota((GROUP_ROWS, 640), 1) == code), hidden[...]).astype(BF16)

    for i in range(FF // 128):
        hidden_t[128 * i : 128 * i + 128, :] = (
            hidden_p[:, 128 * i : 128 * i + 128].astype(F32).T.astype(BF16)
        )
    wanted = routes(ends, order_ref[...].astype(F32))

    for k in range(GROUPS):
        main_code, tail_code = group_codes(y, z, c, k, 1, 16)
        code = jnp.concatenate([main_code, tail_code], axis=0).astype(F32)
        pick[k * GROUP_ROWS : (k + 1) * GROUP_ROWS, :] = onehot(wanted == code)
    stores = [
        pltpu.make_async_copy(src, dst, store_sem.at[i])
        for i, (src, dst) in enumerate(
            [(pick, pick_out), (moment, moment_out), (factor_t, factor_out)]
        )
    ]
    stores[0].start()

    q = q_ref[...]
    loads[2].wait()
    for i in range(3):
        p_part[:, 256 * i : 256 * i + 256] = nt(q, error[256 * i : 256 * i + 256, :])
    loads[3].wait()

    spread = iota((16, 64), 1)
    gathered = iota((16, 64), 0)

    def unpack(ref, k, width, parts, size):
        block = ref[k].astype(F32).reshape(64, width + size)
        main = block[:, :width].astype(BF16)
        tail = block[:, width:].astype(BF16)
        pieces = []
        for i in range(parts):
            at = (gathered // 2) * 8 + 2 * i + gathered % 2
            pieces.append(nn(onehot(spread == at), tail).astype(BF16))
        return main, jnp.concatenate(pieces, axis=1)

    def take(k):
        rows = pl.ds(pl.multiple_of(k * GROUP_ROWS, 16), GROUP_ROWS)
        main, tail = unpack(recv, k, D, 4, 512)
        mine = jnp.concatenate([main, tail], axis=0)
        held[rows, :] = mine
        high, low = split(nt(q, mine))
        both = nn(jnp.concatenate([high, low], axis=0), hidden_p[rows, :])
        p_part[...] += both[:RANK] + both[RANK:]

    def answer(k):
        rows = pl.ds(pl.multiple_of(k * GROUP_ROWS, 16), GROUP_ROWS)
        mine = held[rows, :]
        for i in range(3):
            columns = slice(256 * i, 256 * i + 256)
            slot = nt(mine, weight[columns, :])
            back_send[k, :, :, columns] = slot[:64].reshape(8, 8, 256).astype(BF16)
            tail = slot[64:].astype(BF16)
            to = iota((64, 16), 0)
            at = (to // 8) * 2 + to % 2
            mask = (iota((64, 16), 1) == at) & ((to % 8) // 2 == i)
            placed = nn(onehot(mask), tail)
            if i == 0:
                total = placed
            else:
                total = total + placed
        back_send[k, :, :, FF:] = total.reshape(8, 8, 256).astype(BF16)

    @pl.loop(0, GROUPS - 1)
    def _(k):
        for m in range(MEMBERS):
            forward(k, m).wait_recv()
        take(k)
        answer(k)

    for m in range(MEMBERS - 1):
        forward(GROUPS - 1, m).wait_recv()
    own.wait()
    take(GROUPS - 1)

    def p_scatter(i):
        peer = (replica + i) % NDP
        return pltpu.make_async_remote_copy(
            src_ref=p_part.at[pl.ds(pl.multiple_of(peer * P_ROWS, 8), P_ROWS)],
            dst_ref=p_recv.at[i - 1],
            send_sem=p_sem.at[0, i - 1],
            recv_sem=p_sem.at[1, i - 1],
            device_id={"dp": peer},
            device_id_type=MESH,
        )

    my_rows = pl.ds(pl.multiple_of(replica * P_ROWS, 8), P_ROWS)

    def p_gather(i):
        return pltpu.make_async_remote_copy(
            src_ref=p_full.at[my_rows],
            dst_ref=p_full.at[my_rows],
            send_sem=g_sem.at[0, i - 1],
            recv_sem=g_sem.at[1, i - 1],
            device_id={"dp": (replica + i) % NDP},
            device_id_type=MESH,
        )

    for i in range(1, NDP):
        p_scatter(i).start()

    @pl.loop(0, GROUPS - 1)
    def _(k):
        for m in range(MEMBERS):
            backward(k, m).start()

    answer(GROUPS - 1)
    for m in range(MEMBERS - 1):
        backward(GROUPS - 1, m).start()
    own_back = pltpu.make_async_copy(
        back_send.at[GROUPS - 1, MEMBERS - 1],
        back_recv.at[GROUPS - 1, MEMBERS - 1],
        own_sem.at[1],
    )
    own_back.start()
    for i in range(1, NDP):
        p_scatter(i).wait_recv()
    p_full[my_rows, :] = p_part[my_rows, :] + p_recv[0] + p_recv[1] + p_recv[2]
    for i in range(1, NDP):
        p_gather(i).start()

    @pl.loop(0, D // 256)
    def _(i):
        columns = pl.ds(pl.multiple_of(i * 256, 256), 256)
        value = nn(hidden_t[...], held[:, columns]) + error[:, columns].astype(F32)
        moment[:, columns] = value
        high, low = split(value)
        moment_h[:, columns] = high
        moment_l[:, columns] = low

    stores[1].start()
    for i in range(1, NDP):
        p_gather(i).wait_recv()

    total = p_full[...]
    total_h, total_l = split(total)
    total_both = jnp.concatenate([total_h, total_l], axis=0)

    def z_scatter(i):
        peer = (replica + i) % NDP
        return pltpu.make_async_remote_copy(
            src_ref=z_part.at[i],
            dst_ref=z_recv.at[i - 1],
            send_sem=z_sem.at[0, i - 1],
            recv_sem=z_sem.at[1, i - 1],
            device_id={"dp": peer},
            device_id_type=MESH,
        )

    for i in (2, 1, 3, 0):
        block = pl.ds(pl.multiple_of(((replica + i) % NDP) * BLOCK, BLOCK), BLOCK)
        both = nn(total_both, moment_h[:, block])
        z_part[i] = both[:RANK] + both[RANK:] + nn(total_h, moment_l[:, block])
        if i:
            z_scatter(i).start()

    gram = nt(total, total, lax.Precision.HIGHEST)
    inverse = inverse_factor(gram)
    basis = nn(inverse, total, lax.Precision.HIGHEST)
    p_out[...] = basis
    basis_h, basis_l = split(basis)
    three = jnp.concatenate([basis_h, basis_l, basis_h], axis=0).astype(F32)
    for i in range(FF // 128):
        factor_t[128 * i : 128 * i + 128, :] = three[:, 128 * i : 128 * i + 128].T.astype(BF16)
    stores[2].start()

    for i in range(1, NDP):
        z_scatter(i).wait_recv()
    z_total = z_part[0] + z_recv[0] + z_recv[1] + z_recv[2]
    q_full[replica] = nn(inverse, z_total, lax.Precision.HIGHEST) / NDP

    def q_gather(i):
        return pltpu.make_async_remote_copy(
            src_ref=q_full.at[replica],
            dst_ref=q_full.at[replica],
            send_sem=q_sem.at[0, i - 1],
            recv_sem=q_sem.at[1, i - 1],
            device_id={"dp": (replica + i) % NDP},
            device_id_type=MESH,
        )

    for i in range(1, NDP):
        q_gather(i).start()

    own_back.wait()

    @pl.loop(0, GROUPS - 1)
    def _(k):
        for m in range(MEMBERS):
            backward(k, m).wait_recv()
        rows = pl.ds(pl.multiple_of(k * GROUP_ROWS, 16), GROUP_ROWS)
        main, tail = unpack(back_recv, k, FF, 3, 256)
        back_rows[rows, :] = jnp.concatenate([main, tail], axis=0)

    for m in range(MEMBERS - 1):
        backward(GROUPS - 1, m).wait_recv()
    main, tail = unpack(back_recv, GROUPS - 1, FF, 3, 256)
    back_rows[(GROUPS - 1) * GROUP_ROWS :, :] = jnp.concatenate([main, tail], axis=0)
    for i in range(1, NDP):
        q_gather(i).wait_recv()
    for store in stores:
        store.wait()
    for i in range(1, NDP):
        p_scatter(i).wait_send()
        p_gather(i).wait_send()
        z_scatter(i).wait_send()
        q_gather(i).wait_send()

    @pl.loop(0, GROUPS - 1)
    def _(k):
        for m in range(MEMBERS):
            forward(k, m).wait_send()
            backward(k, m).wait_send()

    for m in range(MEMBERS - 1):
        forward(GROUPS - 1, m).wait_send()
        backward(GROUPS - 1, m).wait_send()


def finish(moment, factor_t, q_part, pick, back_rows, p_in, error_out, q_out, back_out, p_out):
    part = q_part[0]
    q_out[...] = part
    p_out[...] = p_in[...]
    high, low = split(part)
    three = jnp.concatenate([high, high, low], axis=0)
    for j in range(3):
        rows = slice(256 * j, 256 * j + 256)
        error_out[rows, :] = (moment[rows, :] - nn(factor_t[rows, :], three)).astype(BF16)
    chosen = lax.dot_general(
        pick[...], back_rows[...], (((0,), (0,)), ((), ())), preferred_element_type=F32
    )
    back_out[...] = chosen.astype(BF16)


def shards(grad_rows, counts, order, hidden, down_weight, error_in, q_init):
    anywhere = pl.BlockSpec(memory_space=pl.ANY)
    vmem = pl.BlockSpec(memory_space=pltpu.VMEM)
    dma = pltpu.SemaphoreType.DMA
    back_rows, basis, factor, moment, pick, factor_t = pl.pallas_call(
        kernel,
        out_shape=(
            jax.ShapeDtypeStruct((640, FF), BF16),
            jax.ShapeDtypeStruct((RANK, FF), F32),
            jax.ShapeDtypeStruct((NDP, RANK, BLOCK), F32),
            jax.ShapeDtypeStruct((FF, D), F32),
            jax.ShapeDtypeStruct((640, ROWS), BF16),
            jax.ShapeDtypeStruct((FF, 3 * RANK), BF16),
        ),
        in_specs=[anywhere, vmem, vmem, anywhere, anywhere, anywhere, vmem],
        out_specs=(vmem, vmem, vmem, anywhere, anywhere, anywhere),
        scratch_shapes=[
            pltpu.VMEM((ROWS, D), BF16),
            pltpu.VMEM((640, FF), BF16),
            pltpu.VMEM((FF, D), BF16),
            pltpu.VMEM((FF, D), BF16),
            pltpu.VMEM((GROUPS, MEMBERS, 8, WIDE), BF16),
            pltpu.VMEM((GROUPS, MEMBERS, 8, WIDE), BF16),
            pltpu.VMEM((640, D), BF16),
            pltpu.VMEM((640, FF), BF16),
            pltpu.VMEM((FF, 640), BF16),
            pltpu.VMEM((FF, D), F32),
            pltpu.VMEM((FF, D), BF16),
            pltpu.VMEM((FF, D), BF16),
            pltpu.VMEM((640, ROWS), BF16),
            pltpu.VMEM((GROUPS, MEMBERS, 8, BACK), BF16),
            pltpu.VMEM((GROUPS, MEMBERS, 8, BACK), BF16),
            pltpu.VMEM((RANK, FF), F32),
            pltpu.VMEM((NDP - 1, P_ROWS, FF), F32),
            pltpu.VMEM((RANK, FF), F32),
            pltpu.VMEM((NDP, RANK, BLOCK), F32),
            pltpu.VMEM((NDP - 1, RANK, BLOCK), F32),
            pltpu.VMEM((FF, 3 * RANK), BF16),
            dma((4,)),
            dma((3,)),
            dma((GROUPS, MEMBERS)),
            dma((GROUPS, MEMBERS)),
            dma((GROUPS, MEMBERS)),
            dma((GROUPS, MEMBERS)),
            dma((2, NDP - 1)),
            dma((2, NDP - 1)),
            dma((2, NDP - 1)),
            dma((2, NDP - 1)),
            dma((2,)),
        ],
        compiler_params=pltpu.CompilerParams(
            collective_id=0, has_side_effects=True, vmem_limit_bytes=58 << 20
        ),
        name="routed_backward",
    )(
        grad_rows[0],
        counts[0],
        order,
        hidden[0, 0],
        down_weight[0],
        error_in[0, 0],
        q_init[0].T,
    )
    error_new, q_out, back, p_out = pl.pallas_call(
        finish,
        grid=(NDP,),
        out_shape=(
            jax.ShapeDtypeStruct((FF, D), BF16),
            jax.ShapeDtypeStruct((RANK, D), F32),
            jax.ShapeDtypeStruct((ROWS, FF), BF16),
            jax.ShapeDtypeStruct((RANK, FF), F32),
        ),
        in_specs=[
            pl.BlockSpec((FF, BLOCK), lambda i: (0, i)),
            pl.BlockSpec((FF, 3 * RANK), lambda i: (0, 0)),
            pl.BlockSpec((1, RANK, BLOCK), lambda i: (i, 0, 0)),
            pl.BlockSpec((640, ROWS // NDP), lambda i: (0, i)),
            pl.BlockSpec((640, FF), lambda i: (0, 0)),
            pl.BlockSpec((RANK, FF), lambda i: (0, 0)),
        ],
        out_specs=(
            pl.BlockSpec((FF, BLOCK), lambda i: (0, i)),
            pl.BlockSpec((RANK, BLOCK), lambda i: (0, i)),
            pl.BlockSpec((ROWS // NDP, FF), lambda i: (i, 0)),
            pl.BlockSpec((RANK, FF), lambda i: (0, 0)),
        ),
        compiler_params=pltpu.CompilerParams(vmem_limit_bytes=58 << 20),
        name="finish",
    )(moment, factor_t, factor, pick, back_rows, basis)
    return back[None], p_out.T[None], q_out.T[None], error_new[None, None]


def solution(mesh):
    placed = (
        P("dp", "expert", None),
        P("dp", "expert", None),
        P("dp", "expert"),
        P("dp", "expert", None, None),
        P("expert", None, None),
        P("dp", "expert", None, None),
        P("expert", None, None),
    )
    return jax.shard_map(
        shards,
        mesh=mesh,
        in_specs=placed,
        out_specs=(
            P("dp", "expert", None),
            P("expert", None, None),
            P("expert", None, None),
            P("dp", "expert", None, None),
        ),
        check_vma=False,
    )
```

```python
import jax
import jax.numpy as jnp
from jax import lax
from jax.experimental import pallas as pl
from jax.experimental.pallas import tpu as pltpu
from jax.sharding import PartitionSpec as P

MESH = pl.DeviceIdType.MESH
F32 = jnp.float32
BF16 = jnp.bfloat16

NY, NZ, NC, NDP = 4, 8, 2, 4
ROWS, D, FF, RANK, EXPERTS = 512, 2048, 768, 64, 64
GROUPS, MEMBERS = 8, 8
GROUP_ROWS = 80
WIDE = D + 512
BACK = FF + 256
BLOCK = D // NDP
P_ROWS = RANK // NDP
STEPS = 4


def nn(a, b, precision=None):
    return lax.dot_general(
        a, b, (((1,), (0,)), ((), ())), precision=precision, preferred_element_type=F32
    )


def nt(a, b, precision=None):
    return lax.dot_general(
        a, b, (((1,), (1,)), ((), ())), precision=precision, preferred_element_type=F32
    )


def split(a):
    high = a.astype(BF16)
    return high, (a - high.astype(F32)).astype(BF16)


def onehot(mask):
    return jnp.where(mask, 1.0, 0.0).astype(BF16)


def iota(shape, axis):
    return lax.broadcasted_iota(jnp.int32, shape, axis)


def z_step(m):
    half = (m + 1) // 2
    return 4 + (1 - 2 * (m % 2)) * half


def shift(y, z, c, k, m, sign):
    there_y = (y + sign * ((k // 2 + m + 2) % NY) + NY) % NY
    there_z = (z + sign * z_step(m) + NZ) % NZ
    there_c = (c + k + 1) % NC
    return (there_y * NZ + there_z) * NC + there_c


def group_codes(y, z, c, k, sign, scale):
    main = iota((64, 1), 0)
    tail = iota((16, 1), 0)
    main_code = shift(y, z, c, k, main // 8, sign) * scale + main % 8
    tail_code = shift(y, z, c, k, tail // 2, sign) * scale + 8 + tail % 2
    return main_code, tail_code


def routes(ends, rows):
    passed = ends <= rows
    expert = jnp.sum(jnp.where(passed, 1.0, 0.0), axis=0, keepdims=True)
    start = jnp.max(jnp.where(passed, ends, 0.0), axis=0, keepdims=True)
    return expert * 16.0 + (rows - start)


def inverse_factor(gram):
    lanes = iota((RANK, 2 * RANK), 1)
    rows = iota((RANK, 2 * RANK), 0)
    work = jnp.concatenate([gram, jnp.where(iota((RANK, RANK), 0) == iota((RANK, RANK), 1), 1.0, 0.0)], axis=1)
    blocks = [work[8 * b : 8 * b + 8] for b in range(8)]
    below = iota((8, 1), 0)
    for own in range(8):
        columns = [
            [jnp.broadcast_to(blocks[b][:, 8 * own + j : 8 * own + j + 1], (8, 2 * RANK)) for b in range(own, 8)]
            for j in range(8)
        ]
        for j in range(8):
            row = blocks[own][j : j + 1, :]
            inverse = 1.0 / columns[j][0][j : j + 1, :]
            scaled = row * inverse
            for i in range(j + 1, 8):
                across = columns[j][0][i : i + 1, :] * inverse
                columns[i] = [there - here * across for there, here in zip(columns[i], columns[j])]
            for b in range(own, 8):
                factor = columns[j][b - own]
                if b == own:
                    factor = jnp.where(below > j, factor, 0.0)
                blocks[b] = blocks[b] - factor * scaled
    work = jnp.concatenate(blocks, axis=0)
    pivots = jnp.sum(jnp.where(lanes == rows, work, 0.0), axis=1, keepdims=True)
    return work[:, RANK:] * lax.rsqrt(pivots)


def kernel(
    x_hbm, counts_ref, order_ref, hidden_hbm, weight_hbm, error_hbm, q_ref,
    back_rows_out, p_out, q_full, moment_out, pick_out, factor_out,
    x, hidden, weight, error, send, recv, held, hidden_p, hidden_t, moment, moment_h, moment_l,
    pick, back_send, back_recv, p_part, p_recv, p_full, z_part, z_recv, factor_t,
    back_rows, basis_held, load_sem, store_sem, send_sem, recv_sem, back_send_sem, back_recv_sem,
    p_sem, g_sem, z_sem, q_sem, own_sem,
):
    me = lax.axis_index("expert")
    replica = lax.axis_index("dp")
    y, z, c = me // (NZ * NC), (me // NC) % NZ, me % NC

    loads = [
        pltpu.make_async_copy(src, dst, load_sem.at[i])
        for i, (src, dst) in enumerate(
            [(x_hbm, x), (hidden_hbm, hidden), (error_hbm, error), (weight_hbm, weight)]
        )
    ]
    for load in loads:
        load.start()

    barrier = pltpu.get_barrier_semaphore()

    @pl.loop(1, EXPERTS)
    def _(k):
        pl.semaphore_signal(
            barrier, inc=1, device_id={"expert": (me + k) % EXPERTS}, device_id_type=MESH
        )

    for i in range(1, NDP):
        pl.semaphore_signal(
            barrier, inc=1, device_id={"dp": (replica + i) % NDP}, device_id_type=MESH
        )

    counts = counts_ref[...].astype(F32)
    ends = jnp.sum(
        jnp.where(iota((EXPERTS, EXPERTS), 1) <= iota((EXPERTS, EXPERTS), 0), counts, 0.0),
        axis=1,
        keepdims=True,
    )
    codes = routes(ends, iota((1, ROWS), 1).astype(F32))
    loads[0].wait()

    def forward(k, m):
        return pltpu.make_async_remote_copy(
            src_ref=send.at[k, m],
            dst_ref=recv.at[k, m],
            send_sem=send_sem.at[k, m],
            recv_sem=recv_sem.at[k, m],
            device_id={"expert": shift(y, z, c, k, m, 1)},
            device_id_type=MESH,
        )

    def backward(k, m):
        return pltpu.make_async_remote_copy(
            src_ref=back_send.at[k, m],
            dst_ref=back_recv.at[k, m],
            send_sem=back_send_sem.at[k, m],
            recv_sem=back_recv_sem.at[k, m],
            device_id={"expert": shift(y, z, c, k, m, -1)},
            device_id_type=MESH,
        )

    def pack(k):
        rows = iota((64, 1), 0)
        expert = shift(y, z, c, k, rows // 8, 1) * 16
        main = onehot(codes == (expert + rows % 8).astype(F32))
        tail = codes == (expert + 8 + rows % 2).astype(F32)
        part = (rows % 8) // 2
        total = jnp.zeros((64, 512), F32)
        for i in range(4):
            columns = x[:, 512 * i : 512 * i + 512]
            both = nn(
                jnp.concatenate([main, onehot(tail & (part == i))], axis=0), columns
            )
            send[k, :, :, 512 * i : 512 * i + 512] = both[:64].reshape(8, 8, 512).astype(BF16)
            total = total + both[64:]
        send[k, :, :, D:] = total.reshape(8, 8, 512).astype(BF16)

    pack(0)
    pl.semaphore_wait(barrier, EXPERTS - 1 + NDP - 1)
    for m in range(MEMBERS):
        forward(0, m).start()

    @pl.loop(1, GROUPS - 1)
    def _(k):
        pack(k)
        for m in range(MEMBERS):
            forward(k, m).start()

    pack(GROUPS - 1)
    for m in range(MEMBERS - 1):
        forward(GROUPS - 1, m).start()
    own = pltpu.make_async_copy(send.at[GROUPS - 1, MEMBERS - 1], recv.at[GROUPS - 1, MEMBERS - 1], own_sem.at[0])
    own.start()

    loads[1].wait()

    @pl.loop(0, GROUPS)
    def _(k):
        main_code, tail_code = group_codes(y, z, c, k, -1, 10)
        code = jnp.concatenate([main_code, tail_code], axis=0)
        rows = pl.ds(pl.multiple_of(k * GROUP_ROWS, 16), GROUP_ROWS)
        hidden_p[rows, :] = nn(onehot(iota((GROUP_ROWS, 640), 1) == code), hidden[...]).astype(BF16)

    for i in range(FF // 128):
        hidden_t[128 * i : 128 * i + 128, :] = (
            hidden_p[:, 128 * i : 128 * i + 128].astype(F32).T.astype(BF16)
        )
    wanted = routes(ends, order_ref[...].astype(F32))

    places = []
    for k in range(GROUPS):
        main_code, tail_code = group_codes(y, z, c, k, 1, 16)
        code = jnp.concatenate([main_code, tail_code], axis=0).astype(F32)
        places.append(jnp.where(wanted == code, 1.0, 0.0))
    places = jnp.concatenate(places, axis=0)
    for i in range(4):
        pick[128 * i : 128 * i + 128, :] = places[:, 128 * i : 128 * i + 128].T.astype(BF16)
    stores = [
        pltpu.make_async_copy(src, dst, store_sem.at[i])
        for i, (src, dst) in enumerate(
            [(pick, pick_out), (moment, moment_out), (factor_t, factor_out),
             (basis_held, p_out), (back_rows, back_rows_out)]
        )
    ]
    stores[0].start()

    q = q_ref[...]
    loads[2].wait()
    for i in range(3):
        p_part[:, 256 * i : 256 * i + 256] = nt(q, error[256 * i : 256 * i + 256, :])
    loads[3].wait()

    spread = iota((16, 64), 1)
    gathered = iota((16, 64), 0)

    def unpack(ref, k, width, parts, size):
        block = ref[k].astype(F32).reshape(64, width + size)
        main = block[:, :width].astype(BF16)
        tail = block[:, width:].astype(BF16)
        pieces = []
        for i in range(parts):
            at = (gathered // 2) * 8 + 2 * i + gathered % 2
            pieces.append(nn(onehot(spread == at), tail).astype(BF16))
        return main, jnp.concatenate(pieces, axis=1)

    def take(k):
        rows = pl.ds(pl.multiple_of(k * GROUP_ROWS, 16), GROUP_ROWS)
        main, tail = unpack(recv, k, D, 4, 512)
        mine = jnp.concatenate([main, tail], axis=0)
        held[rows, :] = mine
        high, low = split(nt(q, mine))
        both = nn(jnp.concatenate([high, low], axis=0), hidden_p[rows, :])
        p_part[...] += both[:RANK] + both[RANK:]

    def answer(k):
        rows = pl.ds(pl.multiple_of(k * GROUP_ROWS, 16), GROUP_ROWS)
        mine = held[rows, :]
        for i in range(3):
            columns = slice(256 * i, 256 * i + 256)
            slot = nt(mine, weight[columns, :])
            back_send[k, :, :, columns] = slot[:64].reshape(8, 8, 256).astype(BF16)
            tail = slot[64:].astype(BF16)
            to = iota((64, 16), 0)
            at = (to // 8) * 2 + to % 2
            mask = (iota((64, 16), 1) == at) & ((to % 8) // 2 == i)
            placed = nn(onehot(mask), tail)
            if i == 0:
                total = placed
            else:
                total = total + placed
        back_send[k, :, :, FF:] = total.reshape(8, 8, 256).astype(BF16)

    @pl.loop(0, GROUPS - 1)
    def _(k):
        for m in range(MEMBERS):
            forward(k, m).wait_recv()
        take(k)
        answer(k)

    for m in range(MEMBERS - 1):
        forward(GROUPS - 1, m).wait_recv()
    own.wait()
    take(GROUPS - 1)

    def p_scatter(i):
        peer = (replica + i) % NDP
        return pltpu.make_async_remote_copy(
            src_ref=p_part.at[pl.ds(pl.multiple_of(peer * P_ROWS, 8), P_ROWS)],
            dst_ref=p_recv.at[i - 1],
            send_sem=p_sem.at[0, i - 1],
            recv_sem=p_sem.at[1, i - 1],
            device_id={"dp": peer},
            device_id_type=MESH,
        )

    my_rows = pl.ds(pl.multiple_of(replica * P_ROWS, 8), P_ROWS)

    def p_gather(i):
        return pltpu.make_async_remote_copy(
            src_ref=p_full.at[my_rows],
            dst_ref=p_full.at[my_rows],
            send_sem=g_sem.at[0, i - 1],
            recv_sem=g_sem.at[1, i - 1],
            device_id={"dp": (replica + i) % NDP},
            device_id_type=MESH,
        )

    for i in range(1, NDP):
        p_scatter(i).start()

    @pl.loop(0, GROUPS - 1)
    def _(k):
        for m in range(MEMBERS):
            backward(k, m).start()

    answer(GROUPS - 1)
    for m in range(MEMBERS - 1):
        backward(GROUPS - 1, m).start()
    own_back = pltpu.make_async_copy(
        back_send.at[GROUPS - 1, MEMBERS - 1],
        back_recv.at[GROUPS - 1, MEMBERS - 1],
        own_sem.at[1],
    )
    own_back.start()
    for i in range(1, NDP):
        p_scatter(i).wait_recv()
    p_full[my_rows, :] = p_part[my_rows, :] + p_recv[0] + p_recv[1] + p_recv[2]
    for i in range(1, NDP):
        p_gather(i).start()

    @pl.loop(0, D // 256)
    def _(i):
        columns = pl.ds(pl.multiple_of(i * 256, 256), 256)
        value = nn(hidden_t[...], held[:, columns]) + error[:, columns].astype(F32)
        moment[:, columns] = value
        high, low = split(value)
        moment_h[:, columns] = high
        moment_l[:, columns] = low

    stores[1].start()
    for i in range(1, NDP):
        p_gather(i).wait_recv()

    total = p_full[...]
    total_h, total_l = split(total)
    total_both = jnp.concatenate([total_h, total_l], axis=0)

    def z_scatter(i):
        peer = (replica + i) % NDP
        return pltpu.make_async_remote_copy(
            src_ref=z_part.at[i],
            dst_ref=z_recv.at[i - 1],
            send_sem=z_sem.at[0, i - 1],
            recv_sem=z_sem.at[1, i - 1],
            device_id={"dp": peer},
            device_id_type=MESH,
        )

    for i in (2, 1, 3, 0):
        block = pl.ds(pl.multiple_of(((replica + i) % NDP) * BLOCK, BLOCK), BLOCK)
        both = nn(total_both, moment_h[:, block])
        z_part[i] = both[:RANK] + both[RANK:] + nn(total_h, moment_l[:, block])
        if i:
            z_scatter(i).start()

    gram = nt(total, total, lax.Precision.HIGHEST)
    inverse = inverse_factor(gram)
    basis = nn(inverse, total, lax.Precision.HIGHEST)
    basis_held[...] = basis
    stores[3].start()
    basis_h, basis_l = split(basis)
    three = jnp.concatenate([basis_h, basis_l, basis_h], axis=0).astype(F32)
    for i in range(FF // 128):
        factor_t[128 * i : 128 * i + 128, :] = three[:, 128 * i : 128 * i + 128].T.astype(BF16)
    stores[2].start()

    for i in range(1, NDP):
        z_scatter(i).wait_recv()
    z_total = z_part[0] + z_recv[0] + z_recv[1] + z_recv[2]
    q_full[replica] = nn(inverse, z_total, lax.Precision.HIGHEST) / NDP

    def q_gather(i):
        return pltpu.make_async_remote_copy(
            src_ref=q_full.at[replica],
            dst_ref=q_full.at[replica],
            send_sem=q_sem.at[0, i - 1],
            recv_sem=q_sem.at[1, i - 1],
            device_id={"dp": (replica + i) % NDP},
            device_id_type=MESH,
        )

    for i in range(1, NDP):
        q_gather(i).start()

    own_back.wait()

    @pl.loop(0, GROUPS - 1)
    def _(k):
        for m in range(MEMBERS):
            backward(k, m).wait_recv()
        rows = pl.ds(pl.multiple_of(k * GROUP_ROWS, 16), GROUP_ROWS)
        main, tail = unpack(back_recv, k, FF, 3, 256)
        back_rows[rows, :] = jnp.concatenate([main, tail], axis=0)

    for m in range(MEMBERS - 1):
        backward(GROUPS - 1, m).wait_recv()
    main, tail = unpack(back_recv, GROUPS - 1, FF, 3, 256)
    back_rows[(GROUPS - 1) * GROUP_ROWS :, :] = jnp.concatenate([main, tail], axis=0)
    stores[4].start()
    for i in range(1, NDP):
        q_gather(i).wait_recv()
    for store in stores:
        store.wait()
    for i in range(1, NDP):
        p_scatter(i).wait_send()
        p_gather(i).wait_send()
        z_scatter(i).wait_send()
        q_gather(i).wait_send()

    @pl.loop(0, GROUPS - 1)
    def _(k):
        for m in range(MEMBERS):
            forward(k, m).wait_send()
            backward(k, m).wait_send()

    for m in range(MEMBERS - 1):
        forward(GROUPS - 1, m).wait_send()
        backward(GROUPS - 1, m).wait_send()


def finish(moment, factor_t, q_part, pick, back_rows, p_in, error_out, q_out, back_out, p_out, three):
    @pl.when(pl.program_id(0) == 0)
    def _():
        p_out[...] = p_in[...]
        for i in range(NDP):
            part = q_part[i]
            columns = slice(BLOCK * i, BLOCK * i + BLOCK)
            q_out[:, columns] = part
            high, low = split(part)
            three[:, columns] = jnp.concatenate([high, high, low], axis=0)

    for i in range(NDP):
        columns = slice(BLOCK * i, BLOCK * i + BLOCK)
        error_out[:, columns] = (
            moment[:, columns] - nn(factor_t[...], three[:, columns])
        ).astype(BF16)
    back_out[...] = nn(pick[...], back_rows[...]).astype(BF16)


def shards(grad_rows, counts, order, hidden, down_weight, error_in, q_init):
    anywhere = pl.BlockSpec(memory_space=pl.ANY)
    vmem = pl.BlockSpec(memory_space=pltpu.VMEM)
    dma = pltpu.SemaphoreType.DMA
    back_rows, basis, factor, moment, pick, factor_t = pl.pallas_call(
        kernel,
        out_shape=(
            jax.ShapeDtypeStruct((640, FF), BF16),
            jax.ShapeDtypeStruct((RANK, FF), F32),
            jax.ShapeDtypeStruct((NDP, RANK, BLOCK), F32),
            jax.ShapeDtypeStruct((FF, D), F32),
            jax.ShapeDtypeStruct((ROWS, 640), BF16),
            jax.ShapeDtypeStruct((FF, 3 * RANK), BF16),
        ),
        in_specs=[anywhere, vmem, vmem, anywhere, anywhere, anywhere, vmem],
        out_specs=(anywhere, anywhere, vmem, anywhere, anywhere, anywhere),
        scratch_shapes=[
            pltpu.VMEM((ROWS, D), BF16),
            pltpu.VMEM((640, FF), BF16),
            pltpu.VMEM((FF, D), BF16),
            pltpu.VMEM((FF, D), BF16),
            pltpu.VMEM((GROUPS, MEMBERS, 8, WIDE), BF16),
            pltpu.VMEM((GROUPS, MEMBERS, 8, WIDE), BF16),
            pltpu.VMEM((640, D), BF16),
            pltpu.VMEM((640, FF), BF16),
            pltpu.VMEM((FF, 640), BF16),
            pltpu.VMEM((FF, D), F32),
            pltpu.VMEM((FF, D), BF16),
            pltpu.VMEM((FF, D), BF16),
            pltpu.VMEM((ROWS, 640), BF16),
            pltpu.VMEM((GROUPS, MEMBERS, 8, BACK), BF16),
            pltpu.VMEM((GROUPS, MEMBERS, 8, BACK), BF16),
            pltpu.VMEM((RANK, FF), F32),
            pltpu.VMEM((NDP - 1, P_ROWS, FF), F32),
            pltpu.VMEM((RANK, FF), F32),
            pltpu.VMEM((NDP, RANK, BLOCK), F32),
            pltpu.VMEM((NDP - 1, RANK, BLOCK), F32),
            pltpu.VMEM((FF, 3 * RANK), BF16),
            pltpu.VMEM((640, FF), BF16),
            pltpu.VMEM((RANK, FF), F32),
            dma((4,)),
            dma((5,)),
            dma((GROUPS, MEMBERS)),
            dma((GROUPS, MEMBERS)),
            dma((GROUPS, MEMBERS)),
            dma((GROUPS, MEMBERS)),
            dma((2, NDP - 1)),
            dma((2, NDP - 1)),
            dma((2, NDP - 1)),
            dma((2, NDP - 1)),
            dma((2,)),
        ],
        compiler_params=pltpu.CompilerParams(
            collective_id=0, has_side_effects=True, vmem_limit_bytes=58 << 20
        ),
        name="routed_backward",
    )(
        grad_rows[0],
        counts[0],
        order,
        hidden[0, 0],
        down_weight[0],
        error_in[0, 0],
        q_init[0].T,
    )
    error_new, q_out, back, p_out = pl.pallas_call(
        finish,
        grid=(STEPS,),
        out_shape=(
            jax.ShapeDtypeStruct((FF, D), BF16),
            jax.ShapeDtypeStruct((RANK, D), F32),
            jax.ShapeDtypeStruct((ROWS, FF), BF16),
            jax.ShapeDtypeStruct((RANK, FF), F32),
        ),
        in_specs=[
            pl.BlockSpec((FF // STEPS, D), lambda i: (i, 0)),
            pl.BlockSpec((FF // STEPS, 3 * RANK), lambda i: (i, 0)),
            pl.BlockSpec((NDP, RANK, BLOCK), lambda i: (0, 0, 0)),
            pl.BlockSpec((ROWS // STEPS, 640), lambda i: (i, 0)),
            pl.BlockSpec((640, FF), lambda i: (0, 0)),
            pl.BlockSpec((RANK, FF), lambda i: (0, 0)),
        ],
        out_specs=(
            pl.BlockSpec((FF // STEPS, D), lambda i: (i, 0)),
            pl.BlockSpec((RANK, D), lambda i: (0, 0)),
            pl.BlockSpec((ROWS // STEPS, FF), lambda i: (i, 0)),
            pl.BlockSpec((RANK, FF), lambda i: (0, 0)),
        ),
        scratch_shapes=[pltpu.VMEM((3 * RANK, D), BF16)],
        compiler_params=pltpu.CompilerParams(vmem_limit_bytes=58 << 20),
        name="finish",
    )(moment, factor_t, factor, pick, back_rows, basis)
    return back[None], p_out.T[None], q_out.T[None], error_new[None, None]


def solution(mesh):
    placed = (
        P("dp", "expert", None),
        P("dp", "expert", None),
        P("dp", "expert"),
        P("dp", "expert", None, None),
        P("expert", None, None),
        P("dp", "expert", None, None),
        P("expert", None, None),
    )
    return jax.shard_map(
        shards,
        mesh=mesh,
        in_specs=placed,
        out_specs=(
            P("dp", "expert", None),
            P("expert", None, None),
            P("expert", None, None),
            P("dp", "expert", None, None),
        ),
        check_vma=False,
    )
```

```python
import jax
import jax.numpy as jnp
from jax import lax
from jax.experimental import pallas as pl
from jax.experimental.pallas import tpu as pltpu
from jax.sharding import PartitionSpec as P

MESH = pl.DeviceIdType.MESH
F32 = jnp.float32
BF16 = jnp.bfloat16

NY, NZ, NC, NDP = 4, 8, 2, 4
ROWS, D, FF, RANK, EXPERTS = 512, 2048, 768, 64, 64
GROUPS, MEMBERS = 8, 8
GROUP_ROWS = 80
WIDE = D + 512
BACK = FF + 256
BLOCK = D // NDP
HALF = BLOCK // 2
P_ROWS = RANK // NDP
STEPS = 4


def nn(a, b, precision=None):
    return lax.dot_general(
        a, b, (((1,), (0,)), ((), ())), precision=precision, preferred_element_type=F32
    )


def nt(a, b, precision=None):
    return lax.dot_general(
        a, b, (((1,), (1,)), ((), ())), precision=precision, preferred_element_type=F32
    )


def split(a):
    high = a.astype(BF16)
    return high, (a - high.astype(F32)).astype(BF16)


def onehot(mask):
    return jnp.where(mask, 1.0, 0.0).astype(BF16)


def iota(shape, axis):
    return lax.broadcasted_iota(jnp.int32, shape, axis)


def z_step(m):
    half = (m + 1) // 2
    return 4 + (1 - 2 * (m % 2)) * half


def shift(y, z, c, k, m, sign):
    there_y = (y + sign * ((k // 2 + m + 2) % NY) + NY) % NY
    there_z = (z + sign * z_step(m) + NZ) % NZ
    there_c = (c + k + 1) % NC
    return (there_y * NZ + there_z) * NC + there_c


def group_codes(y, z, c, k, sign, scale):
    main = iota((64, 1), 0)
    tail = iota((16, 1), 0)
    main_code = shift(y, z, c, k, main // 8, sign) * scale + main % 8
    tail_code = shift(y, z, c, k, tail // 2, sign) * scale + 8 + tail % 2
    return main_code, tail_code


def routes(ends, rows):
    passed = ends <= rows
    expert = jnp.sum(jnp.where(passed, 1.0, 0.0), axis=0, keepdims=True)
    start = jnp.max(jnp.where(passed, ends, 0.0), axis=0, keepdims=True)
    return expert * 16.0 + (rows - start)


def inverse_factor(gram):
    lanes = iota((RANK, 2 * RANK), 1)
    rows = iota((RANK, 2 * RANK), 0)
    work = jnp.concatenate([gram, jnp.where(iota((RANK, RANK), 0) == iota((RANK, RANK), 1), 1.0, 0.0)], axis=1)
    blocks = [work[8 * b : 8 * b + 8] for b in range(8)]
    below = iota((8, 1), 0)
    for own in range(8):
        columns = [
            [jnp.broadcast_to(blocks[b][:, 8 * own + j : 8 * own + j + 1], (8, 2 * RANK)) for b in range(own, 8)]
            for j in range(8)
        ]
        for j in range(8):
            row = blocks[own][j : j + 1, :]
            inverse = 1.0 / columns[j][0][j : j + 1, :]
            scaled = row * inverse
            for i in range(j + 1, 8):
                across = columns[j][0][i : i + 1, :] * inverse
                columns[i] = [there - here * across for there, here in zip(columns[i], columns[j])]
            for b in range(own, 8):
                factor = columns[j][b - own]
                if b == own:
                    factor = jnp.where(below > j, factor, 0.0)
                blocks[b] = blocks[b] - factor * scaled
    work = jnp.concatenate(blocks, axis=0)
    pivots = jnp.sum(jnp.where(lanes == rows, work, 0.0), axis=1, keepdims=True)
    return work[:, RANK:] * lax.rsqrt(pivots)


def kernel(
    x_hbm, counts_ref, order_ref, hidden_hbm, weight_hbm, error_hbm, q_ref,
    back_rows_out, p_out, q_full, moment_out, pick_out, factor_out,
    x, hidden, weight, error, send, recv, held, hidden_p, hidden_t, moment, moment_h, moment_l,
    pick, back_send, back_recv, p_part, p_recv, p_full, z_part, z_recv, factor_t,
    back_rows, basis_held, load_sem, store_sem, send_sem, recv_sem, back_send_sem, back_recv_sem,
    p_sem, g_sem, z_sem, q_sem, own_sem,
):
    me = lax.axis_index("expert")
    replica = lax.axis_index("dp")
    y, z, c = me // (NZ * NC), (me // NC) % NZ, me % NC

    loads = [
        pltpu.make_async_copy(src, dst, load_sem.at[i])
        for i, (src, dst) in enumerate(
            [(x_hbm, x), (hidden_hbm, hidden), (error_hbm, error), (weight_hbm, weight)]
        )
    ]
    for load in loads:
        load.start()

    barrier = pltpu.get_barrier_semaphore()

    @pl.loop(1, EXPERTS)
    def _(k):
        pl.semaphore_signal(
            barrier, inc=1, device_id={"expert": (me + k) % EXPERTS}, device_id_type=MESH
        )

    for i in range(1, NDP):
        pl.semaphore_signal(
            barrier, inc=1, device_id={"dp": (replica + i) % NDP}, device_id_type=MESH
        )

    counts = counts_ref[...].astype(F32)
    ends = jnp.sum(
        jnp.where(iota((EXPERTS, EXPERTS), 1) <= iota((EXPERTS, EXPERTS), 0), counts, 0.0),
        axis=1,
        keepdims=True,
    )
    codes = routes(ends, iota((1, ROWS), 1).astype(F32))
    loads[0].wait()

    def forward(k, m):
        return pltpu.make_async_remote_copy(
            src_ref=send.at[k, m],
            dst_ref=recv.at[k, m],
            send_sem=send_sem.at[k, m],
            recv_sem=recv_sem.at[k, m],
            device_id={"expert": shift(y, z, c, k, m, 1)},
            device_id_type=MESH,
        )

    def backward(k, m):
        return pltpu.make_async_remote_copy(
            src_ref=back_send.at[k, m],
            dst_ref=back_recv.at[k, m],
            send_sem=back_send_sem.at[k, m],
            recv_sem=back_recv_sem.at[k, m],
            device_id={"expert": shift(y, z, c, k, m, -1)},
            device_id_type=MESH,
        )

    def pack(k):
        rows = iota((64, 1), 0)
        expert = shift(y, z, c, k, rows // 8, 1) * 16
        main = onehot(codes == (expert + rows % 8).astype(F32))
        tail = codes == (expert + 8 + rows % 2).astype(F32)
        part = (rows % 8) // 2
        total = jnp.zeros((64, 512), F32)
        for i in range(4):
            columns = x[:, 512 * i : 512 * i + 512]
            both = nn(
                jnp.concatenate([main, onehot(tail & (part == i))], axis=0), columns
            )
            send[k, :, :, 512 * i : 512 * i + 512] = both[:64].reshape(8, 8, 512).astype(BF16)
            total = total + both[64:]
        send[k, :, :, D:] = total.reshape(8, 8, 512).astype(BF16)

    pack(0)
    pl.semaphore_wait(barrier, EXPERTS - 1 + NDP - 1)
    for m in range(MEMBERS):
        forward(0, m).start()

    @pl.loop(1, GROUPS - 1)
    def _(k):
        pack(k)
        for m in range(MEMBERS):
            forward(k, m).start()

    pack(GROUPS - 1)
    for m in range(MEMBERS - 1):
        forward(GROUPS - 1, m).start()
    own = pltpu.make_async_copy(send.at[GROUPS - 1, MEMBERS - 1], recv.at[GROUPS - 1, MEMBERS - 1], own_sem.at[0])
    own.start()

    loads[1].wait()

    @pl.loop(0, GROUPS)
    def _(k):
        main_code, tail_code = group_codes(y, z, c, k, -1, 10)
        code = jnp.concatenate([main_code, tail_code], axis=0)
        rows = pl.ds(pl.multiple_of(k * GROUP_ROWS, 16), GROUP_ROWS)
        hidden_p[rows, :] = nn(onehot(iota((GROUP_ROWS, 640), 1) == code), hidden[...]).astype(BF16)

    for i in range(FF // 128):
        hidden_t[128 * i : 128 * i + 128, :] = (
            hidden_p[:, 128 * i : 128 * i + 128].astype(F32).T.astype(BF16)
        )
    wanted = routes(ends, order_ref[...].astype(F32))

    places = []
    for k in range(GROUPS):
        main_code, tail_code = group_codes(y, z, c, k, 1, 16)
        code = jnp.concatenate([main_code, tail_code], axis=0).astype(F32)
        places.append(jnp.where(wanted == code, 1.0, 0.0))
    places = jnp.concatenate(places, axis=0)
    for i in range(4):
        pick[128 * i : 128 * i + 128, :] = places[:, 128 * i : 128 * i + 128].T.astype(BF16)
    stores = [
        pltpu.make_async_copy(src, dst, store_sem.at[i])
        for i, (src, dst) in enumerate(
            [(pick, pick_out), (moment, moment_out), (factor_t, factor_out),
             (basis_held, p_out), (back_rows, back_rows_out)]
        )
    ]
    stores[0].start()

    q = q_ref[...]
    loads[2].wait()
    for i in range(3):
        p_part[:, 256 * i : 256 * i + 256] = nt(q, error[256 * i : 256 * i + 256, :])
    loads[3].wait()

    spread = iota((16, 64), 1)
    gathered = iota((16, 64), 0)

    def unpack(ref, k, width, parts, size):
        block = ref[k].astype(F32).reshape(64, width + size)
        main = block[:, :width].astype(BF16)
        tail = block[:, width:].astype(BF16)
        pieces = []
        for i in range(parts):
            at = (gathered // 2) * 8 + 2 * i + gathered % 2
            pieces.append(nn(onehot(spread == at), tail).astype(BF16))
        return main, jnp.concatenate(pieces, axis=1)

    def take(k):
        rows = pl.ds(pl.multiple_of(k * GROUP_ROWS, 16), GROUP_ROWS)
        main, tail = unpack(recv, k, D, 4, 512)
        mine = jnp.concatenate([main, tail], axis=0)
        held[rows, :] = mine
        high, low = split(nt(q, mine))
        both = nn(jnp.concatenate([high, low], axis=0), hidden_p[rows, :])
        p_part[...] += both[:RANK] + both[RANK:]

    def answer(k):
        rows = pl.ds(pl.multiple_of(k * GROUP_ROWS, 16), GROUP_ROWS)
        mine = held[rows, :]
        for i in range(3):
            columns = slice(256 * i, 256 * i + 256)
            slot = nt(mine, weight[columns, :])
            back_send[k, :, :, columns] = slot[:64].reshape(8, 8, 256).astype(BF16)
            tail = slot[64:].astype(BF16)
            to = iota((64, 16), 0)
            at = (to // 8) * 2 + to % 2
            mask = (iota((64, 16), 1) == at) & ((to % 8) // 2 == i)
            placed = nn(onehot(mask), tail)
            if i == 0:
                total = placed
            else:
                total = total + placed
        back_send[k, :, :, FF:] = total.reshape(8, 8, 256).astype(BF16)

    @pl.loop(0, GROUPS - 1)
    def _(k):
        for m in range(MEMBERS):
            forward(k, m).wait_recv()
        take(k)
        answer(k)

    for m in range(MEMBERS - 1):
        forward(GROUPS - 1, m).wait_recv()
    own.wait()
    take(GROUPS - 1)

    def p_scatter(i):
        peer = (replica + i) % NDP
        return pltpu.make_async_remote_copy(
            src_ref=p_part.at[pl.ds(pl.multiple_of(peer * P_ROWS, 8), P_ROWS)],
            dst_ref=p_recv.at[i - 1],
            send_sem=p_sem.at[0, i - 1],
            recv_sem=p_sem.at[1, i - 1],
            device_id={"dp": peer},
            device_id_type=MESH,
        )

    my_rows = pl.ds(pl.multiple_of(replica * P_ROWS, 8), P_ROWS)

    def p_gather(i):
        return pltpu.make_async_remote_copy(
            src_ref=p_full.at[my_rows],
            dst_ref=p_full.at[my_rows],
            send_sem=g_sem.at[0, i - 1],
            recv_sem=g_sem.at[1, i - 1],
            device_id={"dp": (replica + i) % NDP},
            device_id_type=MESH,
        )

    for i in range(1, NDP):
        p_scatter(i).start()

    @pl.loop(0, GROUPS - 1)
    def _(k):
        for m in range(MEMBERS):
            backward(k, m).start()

    answer(GROUPS - 1)
    for m in range(MEMBERS - 1):
        backward(GROUPS - 1, m).start()
    own_back = pltpu.make_async_copy(
        back_send.at[GROUPS - 1, MEMBERS - 1],
        back_recv.at[GROUPS - 1, MEMBERS - 1],
        own_sem.at[1],
    )
    own_back.start()
    for i in range(1, NDP):
        p_scatter(i).wait_recv()
    p_full[my_rows, :] = p_part[my_rows, :] + p_recv[0] + p_recv[1] + p_recv[2]
    for i in range(1, NDP):
        p_gather(i).start()

    @pl.loop(0, D // 256)
    def _(i):
        columns = pl.ds(pl.multiple_of(i * 256, 256), 256)
        value = nn(hidden_t[...], held[:, columns]) + error[:, columns].astype(F32)
        moment[:, columns] = value
        high, low = split(value)
        moment_h[:, columns] = high
        moment_l[:, columns] = low

    stores[1].start()
    for i in range(1, NDP):
        p_gather(i).wait_recv()

    total = p_full[...]
    total_h, total_l = split(total)
    total_both = jnp.concatenate([total_h, total_l], axis=0)

    def z_scatter(h, i):
        peer = (replica + i) % NDP
        return pltpu.make_async_remote_copy(
            src_ref=z_part.at[h, i],
            dst_ref=z_recv.at[h, i - 1],
            send_sem=z_sem.at[h, 0, i - 1],
            recv_sem=z_sem.at[h, 1, i - 1],
            device_id={"dp": peer},
            device_id_type=MESH,
        )

    for h, i in ((0, 2), (0, 1), (0, 3), (1, 2), (1, 1), (1, 3), (0, 0), (1, 0)):
        start = ((replica + i) % NDP) * BLOCK + h * HALF
        block = pl.ds(pl.multiple_of(start, HALF), HALF)
        both = nn(total_both, moment_h[:, block])
        z_part[h, i] = both[:RANK] + both[RANK:] + nn(total_h, moment_l[:, block])
        if i:
            z_scatter(h, i).start()

    gram = nt(total, total, lax.Precision.HIGHEST)
    inverse = inverse_factor(gram)
    basis = nn(inverse, total, lax.Precision.HIGHEST)
    basis_held[...] = basis
    stores[3].start()
    basis_h, basis_l = split(basis)
    three = jnp.concatenate([basis_h, basis_l, basis_h], axis=0).astype(F32)
    for i in range(FF // 128):
        factor_t[128 * i : 128 * i + 128, :] = three[:, 128 * i : 128 * i + 128].T.astype(BF16)
    stores[2].start()

    def q_gather(h, i):
        return pltpu.make_async_remote_copy(
            src_ref=q_full.at[replica, h],
            dst_ref=q_full.at[replica, h],
            send_sem=q_sem.at[h, 0, i - 1],
            recv_sem=q_sem.at[h, 1, i - 1],
            device_id={"dp": (replica + i) % NDP},
            device_id_type=MESH,
        )

    for h in range(2):
        for i in range(1, NDP):
            z_scatter(h, i).wait_recv()
        z_total = z_part[h, 0] + z_recv[h, 0] + z_recv[h, 1] + z_recv[h, 2]
        q_full[replica, h] = nn(inverse, z_total, lax.Precision.HIGHEST) / NDP
        for i in (2, 1, 3):
            q_gather(h, i).start()

    own_back.wait()

    @pl.loop(0, GROUPS - 1)
    def _(k):
        for m in range(MEMBERS):
            backward(k, m).wait_recv()
        rows = pl.ds(pl.multiple_of(k * GROUP_ROWS, 16), GROUP_ROWS)
        main, tail = unpack(back_recv, k, FF, 3, 256)
        back_rows[rows, :] = jnp.concatenate([main, tail], axis=0)

    for m in range(MEMBERS - 1):
        backward(GROUPS - 1, m).wait_recv()
    main, tail = unpack(back_recv, GROUPS - 1, FF, 3, 256)
    back_rows[(GROUPS - 1) * GROUP_ROWS :, :] = jnp.concatenate([main, tail], axis=0)
    stores[4].start()
    for i in range(1, NDP):
        q_gather(0, i).wait_recv()
        q_gather(1, i).wait_recv()
    for store in stores:
        store.wait()
    for i in range(1, NDP):
        p_scatter(i).wait_send()
        p_gather(i).wait_send()
        for h in range(2):
            z_scatter(h, i).wait_send()
            q_gather(h, i).wait_send()

    @pl.loop(0, GROUPS - 1)
    def _(k):
        for m in range(MEMBERS):
            forward(k, m).wait_send()
            backward(k, m).wait_send()

    for m in range(MEMBERS - 1):
        forward(GROUPS - 1, m).wait_send()
        backward(GROUPS - 1, m).wait_send()


def finish(moment, factor_t, q_part, pick, back_rows, p_in, error_out, q_out, back_out, p_out, three):
    @pl.when(pl.program_id(0) == 0)
    def _():
        p_out[...] = p_in[...]
        for i in range(2 * NDP):
            part = q_part[i // 2, i % 2]
            columns = slice(HALF * i, HALF * i + HALF)
            q_out[:, columns] = part
            high, low = split(part)
            three[:, columns] = jnp.concatenate([high, high, low], axis=0)

    for i in range(NDP):
        columns = slice(BLOCK * i, BLOCK * i + BLOCK)
        error_out[:, columns] = (
            moment[:, columns] - nn(factor_t[...], three[:, columns])
        ).astype(BF16)
    back_out[...] = nn(pick[...], back_rows[...]).astype(BF16)


def shards(grad_rows, counts, order, hidden, down_weight, error_in, q_init):
    anywhere = pl.BlockSpec(memory_space=pl.ANY)
    vmem = pl.BlockSpec(memory_space=pltpu.VMEM)
    dma = pltpu.SemaphoreType.DMA
    back_rows, basis, factor, moment, pick, factor_t = pl.pallas_call(
        kernel,
        out_shape=(
            jax.ShapeDtypeStruct((640, FF), BF16),
            jax.ShapeDtypeStruct((RANK, FF), F32),
            jax.ShapeDtypeStruct((NDP, 2, RANK, HALF), F32),
            jax.ShapeDtypeStruct((FF, D), F32),
            jax.ShapeDtypeStruct((ROWS, 640), BF16),
            jax.ShapeDtypeStruct((FF, 3 * RANK), BF16),
        ),
        in_specs=[anywhere, vmem, vmem, anywhere, anywhere, anywhere, vmem],
        out_specs=(anywhere, anywhere, vmem, anywhere, anywhere, anywhere),
        scratch_shapes=[
            pltpu.VMEM((ROWS, D), BF16),
            pltpu.VMEM((640, FF), BF16),
            pltpu.VMEM((FF, D), BF16),
            pltpu.VMEM((FF, D), BF16),
            pltpu.VMEM((GROUPS, MEMBERS, 8, WIDE), BF16),
            pltpu.VMEM((GROUPS, MEMBERS, 8, WIDE), BF16),
            pltpu.VMEM((640, D), BF16),
            pltpu.VMEM((640, FF), BF16),
            pltpu.VMEM((FF, 640), BF16),
            pltpu.VMEM((FF, D), F32),
            pltpu.VMEM((FF, D), BF16),
            pltpu.VMEM((FF, D), BF16),
            pltpu.VMEM((ROWS, 640), BF16),
            pltpu.VMEM((GROUPS, MEMBERS, 8, BACK), BF16),
            pltpu.VMEM((GROUPS, MEMBERS, 8, BACK), BF16),
            pltpu.VMEM((RANK, FF), F32),
            pltpu.VMEM((NDP - 1, P_ROWS, FF), F32),
            pltpu.VMEM((RANK, FF), F32),
            pltpu.VMEM((2, NDP, RANK, HALF), F32),
            pltpu.VMEM((2, NDP - 1, RANK, HALF), F32),
            pltpu.VMEM((FF, 3 * RANK), BF16),
            pltpu.VMEM((640, FF), BF16),
            pltpu.VMEM((RANK, FF), F32),
            dma((4,)),
            dma((5,)),
            dma((GROUPS, MEMBERS)),
            dma((GROUPS, MEMBERS)),
            dma((GROUPS, MEMBERS)),
            dma((GROUPS, MEMBERS)),
            dma((2, NDP - 1)),
            dma((2, NDP - 1)),
            dma((2, 2, NDP - 1)),
            dma((2, 2, NDP - 1)),
            dma((2,)),
        ],
        compiler_params=pltpu.CompilerParams(
            collective_id=0, has_side_effects=True, vmem_limit_bytes=58 << 20
        ),
        name="routed_backward",
    )(
        grad_rows[0],
        counts[0],
        order,
        hidden[0, 0],
        down_weight[0],
        error_in[0, 0],
        q_init[0].T,
    )
    error_new, q_out, back, p_out = pl.pallas_call(
        finish,
        grid=(STEPS,),
        out_shape=(
            jax.ShapeDtypeStruct((FF, D), BF16),
            jax.ShapeDtypeStruct((RANK, D), F32),
            jax.ShapeDtypeStruct((ROWS, FF), BF16),
            jax.ShapeDtypeStruct((RANK, FF), F32),
        ),
        in_specs=[
            pl.BlockSpec((FF // STEPS, D), lambda i: (i, 0)),
            pl.BlockSpec((FF // STEPS, 3 * RANK), lambda i: (i, 0)),
            pl.BlockSpec((NDP, 2, RANK, HALF), lambda i: (0, 0, 0, 0)),
            pl.BlockSpec((ROWS // STEPS, 640), lambda i: (i, 0)),
            pl.BlockSpec((640, FF), lambda i: (0, 0)),
            pl.BlockSpec((RANK, FF), lambda i: (0, 0)),
        ],
        out_specs=(
            pl.BlockSpec((FF // STEPS, D), lambda i: (i, 0)),
            pl.BlockSpec((RANK, D), lambda i: (0, 0)),
            pl.BlockSpec((ROWS // STEPS, FF), lambda i: (i, 0)),
            pl.BlockSpec((RANK, FF), lambda i: (0, 0)),
        ),
        scratch_shapes=[pltpu.VMEM((3 * RANK, D), BF16)],
        compiler_params=pltpu.CompilerParams(vmem_limit_bytes=58 << 20),
        name="finish",
    )(moment, factor_t, factor, pick, back_rows, basis)
    return back[None], p_out.T[None], q_out.T[None], error_new[None, None]


def solution(mesh):
    placed = (
        P("dp", "expert", None),
        P("dp", "expert", None),
        P("dp", "expert"),
        P("dp", "expert", None, None),
        P("expert", None, None),
        P("dp", "expert", None, None),
        P("expert", None, None),
    )
    return jax.shard_map(
        shards,
        mesh=mesh,
        in_specs=placed,
        out_specs=(
            P("dp", "expert", None),
            P("expert", None, None),
            P("expert", None, None),
            P("dp", "expert", None, None),
        ),
        check_vma=False,
    )
```

```python
import jax
import jax.numpy as jnp
from jax import lax
from jax.experimental import pallas as pl
from jax.experimental.pallas import tpu as pltpu
from jax.sharding import PartitionSpec as P

MESH = pl.DeviceIdType.MESH
F32 = jnp.float32
BF16 = jnp.bfloat16

NY, NZ, NC, NDP = 4, 8, 2, 4
ROWS, D, FF, RANK, EXPERTS = 512, 2048, 768, 64, 64
GROUPS, MEMBERS = 8, 8
GROUP_ROWS = 80
WIDE = D + 512
BACK = FF + 256
BLOCK = D // NDP
HALF = BLOCK // 2
P_ROWS = RANK // NDP
STEPS = 4
EARLY = 2


def nn(a, b, precision=None):
    return lax.dot_general(
        a, b, (((1,), (0,)), ((), ())), precision=precision, preferred_element_type=F32
    )


def nt(a, b, precision=None):
    return lax.dot_general(
        a, b, (((1,), (1,)), ((), ())), precision=precision, preferred_element_type=F32
    )


def split(a):
    high = a.astype(BF16)
    return high, (a - high.astype(F32)).astype(BF16)


def onehot(mask):
    return jnp.where(mask, 1.0, 0.0).astype(BF16)


def iota(shape, axis):
    return lax.broadcasted_iota(jnp.int32, shape, axis)


def z_step(m):
    half = (m + 1) // 2
    return 4 + (1 - 2 * (m % 2)) * half


def shift(y, z, c, k, m, sign):
    there_y = (y + sign * ((k // 2 + m + 2) % NY) + NY) % NY
    there_z = (z + sign * z_step(m) + NZ) % NZ
    there_c = (c + k + 1) % NC
    return (there_y * NZ + there_z) * NC + there_c


def group_codes(y, z, c, k, sign, scale):
    main = iota((64, 1), 0)
    tail = iota((16, 1), 0)
    main_code = shift(y, z, c, k, main // 8, sign) * scale + main % 8
    tail_code = shift(y, z, c, k, tail // 2, sign) * scale + 8 + tail % 2
    return main_code, tail_code


def routes(ends, rows):
    passed = ends <= rows
    expert = jnp.sum(jnp.where(passed, 1.0, 0.0), axis=0, keepdims=True)
    start = jnp.max(jnp.where(passed, ends, 0.0), axis=0, keepdims=True)
    return expert * 16.0 + (rows - start)


def inverse_factor(gram):
    lanes = iota((RANK, 2 * RANK), 1)
    rows = iota((RANK, 2 * RANK), 0)
    work = jnp.concatenate([gram, jnp.where(iota((RANK, RANK), 0) == iota((RANK, RANK), 1), 1.0, 0.0)], axis=1)
    blocks = [work[8 * b : 8 * b + 8] for b in range(8)]
    below = iota((8, 1), 0)
    for own in range(8):
        columns = [
            [jnp.broadcast_to(blocks[b][:, 8 * own + j : 8 * own + j + 1], (8, 2 * RANK)) for b in range(own, 8)]
            for j in range(8)
        ]
        for j in range(8):
            row = blocks[own][j : j + 1, :]
            inverse = 1.0 / columns[j][0][j : j + 1, :]
            scaled = row * inverse
            for i in range(j + 1, 8):
                across = columns[j][0][i : i + 1, :] * inverse
                columns[i] = [there - here * across for there, here in zip(columns[i], columns[j])]
            for b in range(own, 8):
                factor = columns[j][b - own]
                if b == own:
                    factor = jnp.where(below > j, factor, 0.0)
                blocks[b] = blocks[b] - factor * scaled
    work = jnp.concatenate(blocks, axis=0)
    pivots = jnp.sum(jnp.where(lanes == rows, work, 0.0), axis=1, keepdims=True)
    return work[:, RANK:] * lax.rsqrt(pivots)


def kernel(
    x_hbm, counts_ref, order_ref, hidden_hbm, weight_hbm, error_hbm, q_ref,
    back_rows_out, p_out, q_full, moment_out, pick_out, factor_out,
    x, hidden, weight, error, send, recv, held, hidden_p, hidden_t, moment, moment_h, moment_l,
    pick, back_send, back_recv, p_part, p_recv, p_full, z_part, z_recv, factor_t,
    back_rows, basis_held, load_sem, store_sem, send_sem, recv_sem, back_send_sem, back_recv_sem,
    p_sem, g_sem, z_sem, q_sem, own_sem,
):
    me = lax.axis_index("expert")
    replica = lax.axis_index("dp")
    y, z, c = me // (NZ * NC), (me // NC) % NZ, me % NC

    loads = [
        pltpu.make_async_copy(src, dst, load_sem.at[i])
        for i, (src, dst) in enumerate(
            [(x_hbm, x), (hidden_hbm, hidden), (error_hbm, error), (weight_hbm, weight)]
        )
    ]
    for load in loads:
        load.start()

    barrier = pltpu.get_barrier_semaphore()

    @pl.loop(1, EXPERTS)
    def _(k):
        pl.semaphore_signal(
            barrier, inc=1, device_id={"expert": (me + k) % EXPERTS}, device_id_type=MESH
        )

    for i in range(1, NDP):
        pl.semaphore_signal(
            barrier, inc=1, device_id={"dp": (replica + i) % NDP}, device_id_type=MESH
        )

    counts = counts_ref[...].astype(F32)
    ends = jnp.sum(
        jnp.where(iota((EXPERTS, EXPERTS), 1) <= iota((EXPERTS, EXPERTS), 0), counts, 0.0),
        axis=1,
        keepdims=True,
    )
    codes = routes(ends, iota((1, ROWS), 1).astype(F32))
    loads[0].wait()

    def forward(k, m):
        return pltpu.make_async_remote_copy(
            src_ref=send.at[k, m],
            dst_ref=recv.at[k, m],
            send_sem=send_sem.at[k, m],
            recv_sem=recv_sem.at[k, m],
            device_id={"expert": shift(y, z, c, k, m, 1)},
            device_id_type=MESH,
        )

    def backward(k, m):
        return pltpu.make_async_remote_copy(
            src_ref=back_send.at[k, m],
            dst_ref=back_recv.at[k, m],
            send_sem=back_send_sem.at[k, m],
            recv_sem=back_recv_sem.at[k, m],
            device_id={"expert": shift(y, z, c, k, m, -1)},
            device_id_type=MESH,
        )

    def pack(k):
        rows = iota((64, 1), 0)
        expert = shift(y, z, c, k, rows // 8, 1) * 16
        main = onehot(codes == (expert + rows % 8).astype(F32))
        tail = codes == (expert + 8 + rows % 2).astype(F32)
        part = (rows % 8) // 2
        total = jnp.zeros((64, 512), F32)
        for i in range(4):
            columns = x[:, 512 * i : 512 * i + 512]
            both = nn(
                jnp.concatenate([main, onehot(tail & (part == i))], axis=0), columns
            )
            send[k, :, :, 512 * i : 512 * i + 512] = both[:64].reshape(8, 8, 512).astype(BF16)
            total = total + both[64:]
        send[k, :, :, D:] = total.reshape(8, 8, 512).astype(BF16)

    pack(0)
    pl.semaphore_wait(barrier, EXPERTS - 1 + NDP - 1)
    for m in range(MEMBERS):
        forward(0, m).start()

    @pl.loop(1, GROUPS - 1)
    def _(k):
        pack(k)
        for m in range(MEMBERS):
            forward(k, m).start()

    pack(GROUPS - 1)
    for m in range(MEMBERS - 1):
        forward(GROUPS - 1, m).start()
    own = pltpu.make_async_copy(send.at[GROUPS - 1, MEMBERS - 1], recv.at[GROUPS - 1, MEMBERS - 1], own_sem.at[0])
    own.start()

    loads[1].wait()

    @pl.loop(0, GROUPS)
    def _(k):
        main_code, tail_code = group_codes(y, z, c, k, -1, 10)
        code = jnp.concatenate([main_code, tail_code], axis=0)
        rows = pl.ds(pl.multiple_of(k * GROUP_ROWS, 16), GROUP_ROWS)
        hidden_p[rows, :] = nn(onehot(iota((GROUP_ROWS, 640), 1) == code), hidden[...]).astype(BF16)

    for i in range(FF // 128):
        hidden_t[128 * i : 128 * i + 128, :] = (
            hidden_p[:, 128 * i : 128 * i + 128].astype(F32).T.astype(BF16)
        )
    wanted = routes(ends, order_ref[...].astype(F32))

    places = []
    for k in range(GROUPS):
        main_code, tail_code = group_codes(y, z, c, k, 1, 16)
        code = jnp.concatenate([main_code, tail_code], axis=0).astype(F32)
        places.append(jnp.where(wanted == code, 1.0, 0.0))
    places = jnp.concatenate(places, axis=0)
    for i in range(4):
        pick[128 * i : 128 * i + 128, :] = places[:, 128 * i : 128 * i + 128].T.astype(BF16)
    stores = [
        pltpu.make_async_copy(src, dst, store_sem.at[i])
        for i, (src, dst) in enumerate(
            [(pick, pick_out), (moment, moment_out), (factor_t, factor_out),
             (basis_held, p_out), (back_rows, back_rows_out)]
        )
    ]
    stores[0].start()

    q = q_ref[...]
    loads[2].wait()
    for i in range(3):
        p_part[:, 256 * i : 256 * i + 256] = nt(q, error[256 * i : 256 * i + 256, :])
    loads[3].wait()

    spread = iota((16, 64), 1)
    gathered = iota((16, 64), 0)

    def unpack(ref, k, width, parts, size):
        block = ref[k].astype(F32).reshape(64, width + size)
        main = block[:, :width].astype(BF16)
        tail = block[:, width:].astype(BF16)
        pieces = []
        for i in range(parts):
            at = (gathered // 2) * 8 + 2 * i + gathered % 2
            pieces.append(nn(onehot(spread == at), tail).astype(BF16))
        return main, jnp.concatenate(pieces, axis=1)

    def take(k):
        rows = pl.ds(pl.multiple_of(k * GROUP_ROWS, 16), GROUP_ROWS)
        main, tail = unpack(recv, k, D, 4, 512)
        mine = jnp.concatenate([main, tail], axis=0)
        held[rows, :] = mine
        high, low = split(nt(q, mine))
        both = nn(jnp.concatenate([high, low], axis=0), hidden_p[rows, :])
        p_part[...] += both[:RANK] + both[RANK:]

    def answer(k):
        rows = pl.ds(pl.multiple_of(k * GROUP_ROWS, 16), GROUP_ROWS)
        mine = held[rows, :]
        for i in range(3):
            columns = slice(256 * i, 256 * i + 256)
            slot = nt(mine, weight[columns, :])
            back_send[k, :, :, columns] = slot[:64].reshape(8, 8, 256).astype(BF16)
            tail = slot[64:].astype(BF16)
            to = iota((64, 16), 0)
            at = (to // 8) * 2 + to % 2
            mask = (iota((64, 16), 1) == at) & ((to % 8) // 2 == i)
            placed = nn(onehot(mask), tail)
            if i == 0:
                total = placed
            else:
                total = total + placed
        back_send[k, :, :, FF:] = total.reshape(8, 8, 256).astype(BF16)

    @pl.loop(0, GROUPS - 1 - EARLY)
    def _(k):
        for m in range(MEMBERS):
            forward(k, m).wait_recv()
        take(k)
        answer(k)

    @pl.loop(GROUPS - 1 - EARLY, GROUPS - 1)
    def _(k):
        for m in range(MEMBERS):
            forward(k, m).wait_recv()
        take(k)
        answer(k)
        for m in range(MEMBERS):
            backward(k - (GROUPS - 1 - EARLY), m).start()

    for m in range(MEMBERS - 1):
        forward(GROUPS - 1, m).wait_recv()
    own.wait()
    take(GROUPS - 1)

    def p_scatter(i):
        peer = (replica + i) % NDP
        return pltpu.make_async_remote_copy(
            src_ref=p_part.at[pl.ds(pl.multiple_of(peer * P_ROWS, 8), P_ROWS)],
            dst_ref=p_recv.at[i - 1],
            send_sem=p_sem.at[0, i - 1],
            recv_sem=p_sem.at[1, i - 1],
            device_id={"dp": peer},
            device_id_type=MESH,
        )

    my_rows = pl.ds(pl.multiple_of(replica * P_ROWS, 8), P_ROWS)

    def p_gather(i):
        return pltpu.make_async_remote_copy(
            src_ref=p_full.at[my_rows],
            dst_ref=p_full.at[my_rows],
            send_sem=g_sem.at[0, i - 1],
            recv_sem=g_sem.at[1, i - 1],
            device_id={"dp": (replica + i) % NDP},
            device_id_type=MESH,
        )

    for i in range(1, NDP):
        p_scatter(i).start()

    @pl.loop(EARLY, GROUPS - 1)
    def _(k):
        for m in range(MEMBERS):
            backward(k, m).start()

    answer(GROUPS - 1)
    for m in range(MEMBERS - 1):
        backward(GROUPS - 1, m).start()
    own_back = pltpu.make_async_copy(
        back_send.at[GROUPS - 1, MEMBERS - 1],
        back_recv.at[GROUPS - 1, MEMBERS - 1],
        own_sem.at[1],
    )
    own_back.start()
    for i in range(1, NDP):
        p_scatter(i).wait_recv()
    p_full[my_rows, :] = p_part[my_rows, :] + p_recv[0] + p_recv[1] + p_recv[2]
    for i in range(1, NDP):
        p_gather(i).start()

    @pl.loop(0, D // 256)
    def _(i):
        columns = pl.ds(pl.multiple_of(i * 256, 256), 256)
        value = nn(hidden_t[...], held[:, columns]) + error[:, columns].astype(F32)
        moment[:, columns] = value
        high, low = split(value)
        moment_h[:, columns] = high
        moment_l[:, columns] = low

    stores[1].start()
    for i in range(1, NDP):
        p_gather(i).wait_recv()

    total = p_full[...]
    total_h, total_l = split(total)
    total_both = jnp.concatenate([total_h, total_l], axis=0)

    def z_scatter(h, i):
        peer = (replica + i) % NDP
        return pltpu.make_async_remote_copy(
            src_ref=z_part.at[h, i],
            dst_ref=z_recv.at[h, i - 1],
            send_sem=z_sem.at[h, 0, i - 1],
            recv_sem=z_sem.at[h, 1, i - 1],
            device_id={"dp": peer},
            device_id_type=MESH,
        )

    for h, i in ((0, 2), (0, 1), (0, 3), (1, 2), (1, 1), (1, 3), (0, 0), (1, 0)):
        start = ((replica + i) % NDP) * BLOCK + h * HALF
        block = pl.ds(pl.multiple_of(start, HALF), HALF)
        both = nn(total_both, moment_h[:, block])
        z_part[h, i] = both[:RANK] + both[RANK:] + nn(total_h, moment_l[:, block])
        if i:
            z_scatter(h, i).start()

    gram = nt(total, total, lax.Precision.HIGHEST)
    inverse = inverse_factor(gram)
    basis = nn(inverse, total, lax.Precision.HIGHEST)
    basis_held[...] = basis
    stores[3].start()
    basis_h, basis_l = split(basis)
    three = jnp.concatenate([basis_h, basis_l, basis_h], axis=0).astype(F32)
    for i in range(FF // 128):
        factor_t[128 * i : 128 * i + 128, :] = three[:, 128 * i : 128 * i + 128].T.astype(BF16)
    stores[2].start()

    def q_gather(h, i):
        return pltpu.make_async_remote_copy(
            src_ref=q_full.at[replica, h],
            dst_ref=q_full.at[replica, h],
            send_sem=q_sem.at[h, 0, i - 1],
            recv_sem=q_sem.at[h, 1, i - 1],
            device_id={"dp": (replica + i) % NDP},
            device_id_type=MESH,
        )

    for h in range(2):
        for i in range(1, NDP):
            z_scatter(h, i).wait_recv()
        z_total = z_part[h, 0] + z_recv[h, 0] + z_recv[h, 1] + z_recv[h, 2]
        q_full[replica, h] = nn(inverse, z_total, lax.Precision.HIGHEST) / NDP
        for i in (2, 1, 3):
            q_gather(h, i).start()

    own_back.wait()

    @pl.loop(0, GROUPS - 1)
    def _(k):
        for m in range(MEMBERS):
            backward(k, m).wait_recv()
        rows = pl.ds(pl.multiple_of(k * GROUP_ROWS, 16), GROUP_ROWS)
        main, tail = unpack(back_recv, k, FF, 3, 256)
        back_rows[rows, :] = jnp.concatenate([main, tail], axis=0)

    for m in range(MEMBERS - 1):
        backward(GROUPS - 1, m).wait_recv()
    main, tail = unpack(back_recv, GROUPS - 1, FF, 3, 256)
    back_rows[(GROUPS - 1) * GROUP_ROWS :, :] = jnp.concatenate([main, tail], axis=0)
    stores[4].start()
    for i in range(1, NDP):
        q_gather(0, i).wait_recv()
        q_gather(1, i).wait_recv()
    for store in stores:
        store.wait()
    for i in range(1, NDP):
        p_scatter(i).wait_send()
        p_gather(i).wait_send()
        for h in range(2):
            z_scatter(h, i).wait_send()
            q_gather(h, i).wait_send()

    @pl.loop(0, GROUPS - 1)
    def _(k):
        for m in range(MEMBERS):
            forward(k, m).wait_send()
            backward(k, m).wait_send()

    for m in range(MEMBERS - 1):
        forward(GROUPS - 1, m).wait_send()
        backward(GROUPS - 1, m).wait_send()


def finish(moment, factor_t, q_part, pick, back_rows, p_in, error_out, q_out, back_out, p_out, three):
    @pl.when(pl.program_id(0) == 0)
    def _():
        p_out[...] = p_in[...]
        for i in range(2 * NDP):
            part = q_part[i // 2, i % 2]
            columns = slice(HALF * i, HALF * i + HALF)
            q_out[:, columns] = part
            high, low = split(part)
            three[:, columns] = jnp.concatenate([high, high, low], axis=0)

    for i in range(NDP):
        columns = slice(BLOCK * i, BLOCK * i + BLOCK)
        error_out[:, columns] = (
            moment[:, columns] - nn(factor_t[...], three[:, columns])
        ).astype(BF16)
    back_out[...] = nn(pick[...], back_rows[...]).astype(BF16)


def shards(grad_rows, counts, order, hidden, down_weight, error_in, q_init):
    anywhere = pl.BlockSpec(memory_space=pl.ANY)
    vmem = pl.BlockSpec(memory_space=pltpu.VMEM)
    dma = pltpu.SemaphoreType.DMA
    back_rows, basis, factor, moment, pick, factor_t = pl.pallas_call(
        kernel,
        out_shape=(
            jax.ShapeDtypeStruct((640, FF), BF16),
            jax.ShapeDtypeStruct((RANK, FF), F32),
            jax.ShapeDtypeStruct((NDP, 2, RANK, HALF), F32),
            jax.ShapeDtypeStruct((FF, D), F32),
            jax.ShapeDtypeStruct((ROWS, 640), BF16),
            jax.ShapeDtypeStruct((FF, 3 * RANK), BF16),
        ),
        in_specs=[anywhere, vmem, vmem, anywhere, anywhere, anywhere, vmem],
        out_specs=(anywhere, anywhere, vmem, anywhere, anywhere, anywhere),
        scratch_shapes=[
            pltpu.VMEM((ROWS, D), BF16),
            pltpu.VMEM((640, FF), BF16),
            pltpu.VMEM((FF, D), BF16),
            pltpu.VMEM((FF, D), BF16),
            pltpu.VMEM((GROUPS, MEMBERS, 8, WIDE), BF16),
            pltpu.VMEM((GROUPS, MEMBERS, 8, WIDE), BF16),
            pltpu.VMEM((640, D), BF16),
            pltpu.VMEM((640, FF), BF16),
            pltpu.VMEM((FF, 640), BF16),
            pltpu.VMEM((FF, D), F32),
            pltpu.VMEM((FF, D), BF16),
            pltpu.VMEM((FF, D), BF16),
            pltpu.VMEM((ROWS, 640), BF16),
            pltpu.VMEM((GROUPS, MEMBERS, 8, BACK), BF16),
            pltpu.VMEM((GROUPS, MEMBERS, 8, BACK), BF16),
            pltpu.VMEM((RANK, FF), F32),
            pltpu.VMEM((NDP - 1, P_ROWS, FF), F32),
            pltpu.VMEM((RANK, FF), F32),
            pltpu.VMEM((2, NDP, RANK, HALF), F32),
            pltpu.VMEM((2, NDP - 1, RANK, HALF), F32),
            pltpu.VMEM((FF, 3 * RANK), BF16),
            pltpu.VMEM((640, FF), BF16),
            pltpu.VMEM((RANK, FF), F32),
            dma((4,)),
            dma((5,)),
            dma((GROUPS, MEMBERS)),
            dma((GROUPS, MEMBERS)),
            dma((GROUPS, MEMBERS)),
            dma((GROUPS, MEMBERS)),
            dma((2, NDP - 1)),
            dma((2, NDP - 1)),
            dma((2, 2, NDP - 1)),
            dma((2, 2, NDP - 1)),
            dma((2,)),
        ],
        compiler_params=pltpu.CompilerParams(
            collective_id=0, has_side_effects=True, vmem_limit_bytes=58 << 20
        ),
        name="routed_backward",
    )(
        grad_rows[0],
        counts[0],
        order,
        hidden[0, 0],
        down_weight[0],
        error_in[0, 0],
        q_init[0].T,
    )
    error_new, q_out, back, p_out = pl.pallas_call(
        finish,
        grid=(STEPS,),
        out_shape=(
            jax.ShapeDtypeStruct((FF, D), BF16),
            jax.ShapeDtypeStruct((RANK, D), F32),
            jax.ShapeDtypeStruct((ROWS, FF), BF16),
            jax.ShapeDtypeStruct((RANK, FF), F32),
        ),
        in_specs=[
            pl.BlockSpec((FF // STEPS, D), lambda i: (i, 0)),
            pl.BlockSpec((FF // STEPS, 3 * RANK), lambda i: (i, 0)),
            pl.BlockSpec((NDP, 2, RANK, HALF), lambda i: (0, 0, 0, 0)),
            pl.BlockSpec((ROWS // STEPS, 640), lambda i: (i, 0)),
            pl.BlockSpec((640, FF), lambda i: (0, 0)),
            pl.BlockSpec((RANK, FF), lambda i: (0, 0)),
        ],
        out_specs=(
            pl.BlockSpec((FF // STEPS, D), lambda i: (i, 0)),
            pl.BlockSpec((RANK, D), lambda i: (0, 0)),
            pl.BlockSpec((ROWS // STEPS, FF), lambda i: (i, 0)),
            pl.BlockSpec((RANK, FF), lambda i: (0, 0)),
        ),
        scratch_shapes=[pltpu.VMEM((3 * RANK, D), BF16)],
        compiler_params=pltpu.CompilerParams(vmem_limit_bytes=58 << 20),
        name="finish",
    )(moment, factor_t, factor, pick, back_rows, basis)
    return back[None], p_out.T[None], q_out.T[None], error_new[None, None]


def solution(mesh):
    placed = (
        P("dp", "expert", None),
        P("dp", "expert", None),
        P("dp", "expert"),
        P("dp", "expert", None, None),
        P("expert", None, None),
        P("dp", "expert", None, None),
        P("expert", None, None),
    )
    return jax.shard_map(
        shards,
        mesh=mesh,
        in_specs=placed,
        out_specs=(
            P("dp", "expert", None),
            P("expert", None, None),
            P("expert", None, None),
            P("dp", "expert", None, None),
        ),
        check_vma=False,
    )
```
